32 devices in a mesh: wide: 8 (over z, x), chol: 4 (over y, core).
Axes of the slice: x: 2, y: 2, z: 4, core: 2. Of those that a mesh axis runs over, the one named last changes fastest.
Arguments:
- walkers: bfloat16 [8, 2048, 256], P('wide', 'chol'), may hold values from -6 to 6
- intersection_inv: bfloat16 [8, 256, 256], P('wide'), may hold values from -0.375 to 0.375
- trial_state: bfloat16 [2048, 256], replicated, may hold values from -0.125 to 0.125
- chol_tiles: bfloat16 [2048, 128, 128], P(('wide', 'chol')), may hold values from -1.25 to 1.25
- tile_vector: int32 [2048], P(('wide', 'chol')), may hold values from 0 to 63
- tile_row: int32 [2048], P(('wide', 'chol')), may hold values from 0 to 15
- tile_col: int32 [2048], P(('wide', 'chol')), may hold values from 0 to 3
- tile_count: int32 [32], P(('wide', 'chol')), may hold values from 32 to 64, as said below
- sources: int32 [8], replicated, may hold values from 0 to 7
- aux_noise: float32 [8, 512], P(None, 'wide'), may hold values from -6 to 6
Outputs:
- force_bias: float32 [8, 512], P(None, 'wide')
- new_walkers: bfloat16 [8, 2048, 256], P('wide', 'chol')
The draws below stay inside these ranges and needn't reach their ends.
Inputs may be any that keep to these rules, and one draw needn't show every extreme that they name: `tile_count`: slots beyond a device's count are ignored; some device has all 64 slots live.
All inputs are finite; a program needn't handle non-finite values.
Results may differ from the reference program's by a relative error of at most 0.019.
Values may be sent and summed in bfloat16 or wider, within the bound.
A program may use at most 192 MiB of HBM per device.

```python
import jax
import jax.numpy as jnp
from jax import lax

ORB = 2048
NEL = 256
TB = 128
TAYLOR = 4
VEC_DEV = 64
TILE_CAP = 64
WALKERS = 8
VEC = 512
ORB_DEV = 512
NTILE = 16
COLBLK = 4
N_CHOL = 4
DEVICES = 32


def draw_tile_count(key, part):
    first, second = jax.random.split(key)
    counts = jax.random.randint(first, (DEVICES,), TILE_CAP // 2, TILE_CAP + 1)
    where = jax.random.randint(second, (), 0, DEVICES)
    return jnp.where(jnp.arange(DEVICES) == where, TILE_CAP, counts).astype(jnp.int32)


def plant(drawn, own_key, smallest, high):
    longest = drawn.shape.index(max(drawn.shape))
    spots = []
    for shift in (0, 1):
        where = [jax.random.randint(jax.random.fold_in(own_key, axis), (), 0, length) for axis, length in enumerate(drawn.shape)]
        where[longest] = (where[longest] + shift) % drawn.shape[longest]
        spots.append(tuple(where))
    return drawn.at[spots[0]].set(smallest).at[spots[1]].set(high)


def steps_of(own_key, extent, cuts, low, largest):
    factor_of = 1.0
    for position, blocks in cuts:
        steps = jax.random.uniform(jax.random.fold_in(jax.random.fold_in(own_key, 6), position), (blocks,), jnp.float32, low / len(cuts), largest / len(cuts))
        factor_of = factor_of * jnp.repeat(jnp.exp(steps), extent[position] // blocks).reshape((-1,) + (1,) * (len(extent) - 1 - position))
    return factor_of


def normal_values(key, dims, scale, most, shards=(), kind=jnp.bfloat16):
    gain = steps_of(key, dims, shards, -0.22, 0.18) if shards else 1.0
    array = jax.random.normal(key, dims, jnp.float32) * scale * gain
    return jnp.minimum(jnp.maximum(array, -most), most).astype(kind)


def setup_inputs(seed: int = 0) -> dict:
    arg_keys = jax.random.split(jax.random.key(seed), 11)
    return {
        "walkers": normal_values(arg_keys[0], (WALKERS, ORB, NEL), 1.0, 6.0, ((0, 8), (1, 4))),
        "intersection_inv": normal_values(arg_keys[1], (WALKERS, NEL, NEL), NEL ** -0.5, 0.375, ((0, 8),)),
        "trial_state": normal_values(arg_keys[2], (ORB, NEL), ORB ** -0.5, 0.125),
        "chol_tiles": normal_values(arg_keys[3], (TILE_CAP * DEVICES, TB, TB), (10 * ORB * TB ** -1 * (ORB * TILE_CAP * DEVICES) ** -0.5), 1.25, ((0, 32),)),
        "tile_vector": plant(jax.random.randint(arg_keys[4], (TILE_CAP * DEVICES,), 0, VEC_DEV), jax.random.fold_in(arg_keys[4], 1), 0, VEC_DEV - 1).astype(jnp.int32),
        "tile_row": plant(jax.random.randint(arg_keys[5], (TILE_CAP * DEVICES,), 0, NTILE), jax.random.fold_in(arg_keys[5], 1), 0, NTILE - 1).astype(jnp.int32),
        "tile_col": plant(jax.random.randint(arg_keys[6], (TILE_CAP * DEVICES,), 0, COLBLK), jax.random.fold_in(arg_keys[6], 1), 0, COLBLK - 1).astype(jnp.int32),
        "tile_count": draw_tile_count(jax.random.fold_in(arg_keys[10], 71), 0),
        "sources": plant(jax.random.randint(arg_keys[8], (WALKERS,), 0, WALKERS), jax.random.fold_in(arg_keys[8], 1), 0, WALKERS - 1).astype(jnp.int32),
        "aux_noise": normal_values(arg_keys[9], (WALKERS, VEC), 1.0, 6.0, ((1, 8),), jnp.float32),
    }


SQRT_TAU = 0.1


def reference(walkers, intersection_inv, trial_state, chol_tiles, tile_vector, tile_row, tile_col, tile_count, sources, aux_noise):
    f32 = jnp.float32
    bf16 = jnp.bfloat16
    theta = jnp.einsum('wmn,wnk->wmk', walkers.astype(f32), intersection_inv.astype(f32)).astype(bf16)
    theta_new = jnp.take(theta, sources, axis=0)
    picked = jnp.take(walkers, sources, axis=0)
    trial_blocks = trial_state.reshape(NTILE, TB, NEL)
    slots = jnp.arange(TILE_CAP * DEVICES, dtype=jnp.int32)
    device = slots // TILE_CAP
    live = ((slots % TILE_CAP) < jnp.take(tile_count, device)).astype(f32)
    columns = (device % N_CHOL) * COLBLK + tile_col
    vectors = (device // N_CHOL) * VEC_DEV + tile_vector
    zero = jnp.zeros((), jnp.int32)

    def bias_step(total, item):
        tile, row, column, vector, weight = item
        rows_here = lax.dynamic_index_in_dim(trial_blocks, row, 0, keepdims=False)
        projected = jnp.dot(tile.T, rows_here, preferred_element_type=f32).astype(bf16)
        projected = lax.optimization_barrier(projected).astype(f32)
        block = lax.dynamic_slice(theta_new, (zero, column * TB, zero), (WALKERS, TB, NEL)).astype(f32)
        value = jnp.sum(block * projected[None], axis=(1, 2)) * weight
        return total.at[:, vector].add(value), None

    force_bias, _ = lax.scan(bias_step, jnp.zeros((WALKERS, VEC), f32),
                             (chol_tiles, tile_row, columns, vectors, live))
    field = (aux_noise - SQRT_TAU * force_bias).astype(bf16)
    field_wide = field.astype(f32)

    def device_step(operator, item):
        tiles_here, rows_here, cols_here, vecs_here, live_here, chol_index = item

        def tile_step(part, inner):
            tile, row, column, vector, weight = inner
            coef = lax.dynamic_index_in_dim(field_wide, vector, 1, keepdims=False) * weight
            start = (zero, row * TB, column * TB)
            block = lax.dynamic_slice(part, start, (WALKERS, TB, TB)) + coef[:, None, None] * tile.astype(f32)[None]
            return lax.dynamic_update_slice(part, block, start), None

        part, _ = lax.scan(tile_step, jnp.zeros((WALKERS, ORB, ORB_DEV), f32),
                           (tiles_here, rows_here, cols_here, vecs_here, live_here))
        rounded = lax.optimization_barrier(part.astype(bf16)).astype(f32)
        start = (zero, zero, chol_index * ORB_DEV)
        merged = lax.dynamic_slice(operator, start, (WALKERS, ORB, ORB_DEV)) + rounded
        return lax.dynamic_update_slice(operator, merged, start), None

    items = (chol_tiles.reshape(DEVICES, TILE_CAP, TB, TB), tile_row.reshape(DEVICES, TILE_CAP),
             tile_col.reshape(DEVICES, TILE_CAP), vectors.reshape(DEVICES, TILE_CAP),
             live.reshape(DEVICES, TILE_CAP), jnp.arange(DEVICES, dtype=jnp.int32) % N_CHOL)
    operator, _ = lax.scan(device_step, jnp.zeros((WALKERS, ORB, ORB), f32), items)
    operator = lax.optimization_barrier(operator.astype(bf16)).astype(f32)
    term = picked
    total = picked.astype(f32)
    for order in range(1, TAYLOR + 1):
        product = jnp.einsum('wpq,wqn->wpn', operator, term.astype(f32))
        term = (SQRT_TAU / order * product).astype(bf16)
        total = total + term.astype(f32)
    return force_bias, total.astype(bf16)
```

```python
import functools

import jax
import jax.numpy as jnp
from jax import lax
from jax.experimental import pallas as pl
from jax.experimental.pallas import tpu as pltpu
from jax.sharding import PartitionSpec as P

TAYLOR = 4


SQRT_TAU = 0.1
MESH = pl.DeviceIdType.MESH
VMEM_LIMIT = 56 * 1024 * 1024


def split_wide(wide, tile_size):
    parts = min(wide // 2, tile_size // 16)
    return parts, wide // parts


def remote(src, dst, send, recv, device):
    return pltpu.make_async_remote_copy(
        src_ref=src, dst_ref=dst, send_sem=send, recv_sem=recv, device_id=device, device_id_type=MESH
    )


def meet(peers):
    barrier = pltpu.get_barrier_semaphore()
    for peer in peers:
        pl.semaphore_signal(barrier, inc=1, device_id=peer, device_id_type=MESH)
    return lambda: pl.semaphore_wait(barrier, len(peers))


def gather_kernel(
    nr,
    ng,
    nc,
    row_s,
    col_s,
    count_s,
    src_s,
    walk_ref,
    inv_ref,
    trial_ref,
    tiles_ref,
    cut_ref,
    noise_ref,
    meta_ref,
    force_ref,
    coef_ref,
    picked_ref,
    tin_ref,
    blk,
    inv_all,
    proj,
    theta,
    scores,
    score,
    bias_in,
    sent,
    got,
    wz_s,
    wz_r,
    wx_s,
    wx_r,
    iq_s,
    iq_r,
    tz_s,
    tz_r,
    tx_s,
    tx_r,
    own_s,
    b_s,
    b_r,
    c_s,
    c_r,
):
    f32 = jnp.float32
    bf16 = jnp.bfloat16
    nw = nr * ng
    a = lax.axis_index("wide")
    c = lax.axis_index("chol")
    z = a // ng
    x = a % ng
    orb = walk_ref.shape[0]
    nel = walk_ref.shape[1]
    q = nel // nc
    slots, tb, _ = tiles_ref.shape
    walk_all, vec = noise_ref.shape
    group = walk_all // ng
    cols = orb // tb

    def slab(d, e):
        return ((z + nr - d) % nr) * ng + (x + ng - e) % ng

    def z_peer(d):
        return (((z + d) % nr) * ng + x, c)

    def x_peer(e):
        return (z * ng + (x + e) % ng, c)

    def c_peer(e):
        return (a, (c + e) % nc)

    def w_peer(f):
        return ((a + f) % nw, c)

    wait_all = meet([w_peer(f) for f in range(1, nw)] + [c_peer(e) for e in range(1, nc)])
    q_at = pl.ds(pl.multiple_of(c * q, 16), q)
    blk[a, pl.ds(0, orb), :] = walk_ref[...]
    blk[a, pl.ds(orb, q), :] = inv_ref[q_at, :]
    wait_all()

    wz = []
    wx = {}
    tz = []
    tx = {}
    iq = []

    def walk_x(d):
        for e in range(1, ng):
            at = blk.at[slab(d, 0)]
            wx[d, e] = remote(at, at, wx_s.at[e - 1, d], wx_r.at[e - 1, d], x_peer(e))
            wx[d, e].start()

    def tile_at(s):
        return tin_ref.at[:, pl.ds(pl.multiple_of(s * slots, slots), slots), :]

    def tile_x(d):
        for e in range(1, ng):
            at = tile_at(slab(d, 0))
            src = cut_ref.at[z] if d == 0 else at
            tx[d, e] = remote(src, at, tx_s.at[e - 1, d], tx_r.at[e - 1, d], x_peer(e))
            tx[d, e].start()

    def inverse(d, e):
        s = slab(d, e)
        inv_all[s, q_at, :] = blk[s, pl.ds(orb, q), :]
        for f in range(1, nc):
            copy = remote(
                blk.at[s, pl.ds(orb, q)],
                inv_all.at[s, q_at],
                iq_s.at[d, e, f - 1],
                iq_r.at[d, e, f - 1],
                c_peer(f),
            )
            copy.start()
            iq.append(copy)

    for d in range(1, nr):
        at = blk.at[a]
        copy = remote(at, at, wz_s.at[d - 1], wz_r.at[d - 1], z_peer(d))
        copy.start()
        wz.append(copy)
    walk_x(0)
    for d in range(1, nr):
        copy = remote(
            cut_ref.at[(z + d) % nr], tile_at(a), tz_s.at[d - 1], tz_r.at[d - 1], z_peer(d)
        )
        copy.start()
        tz.append(copy)
    own = pltpu.make_async_copy(cut_ref.at[z], tile_at(a), own_s)
    own.start()
    inverse(0, 0)

    def project(i, carry):
        rows = trial_ref[row_s[i]]
        out = lax.dot_general(tiles_ref[i], rows, (((0,), (0,)), ((), ())), preferred_element_type=f32)
        proj[i] = out.astype(bf16)
        return carry

    cuts = [slots * d // nr for d in range(nr + 1)]
    for d in range(1, nr):
        lax.fori_loop(cuts[d - 1], cuts[d], project, 0)
        wz[d - 1].wait_recv()
        walk_x(d)
        inverse(d, 0)
    lax.fori_loop(cuts[nr - 1], cuts[nr], project, 0)
    tile_x(0)
    for d in range(nr):
        for e in range(1, ng):
            wx[d, e].wait_recv()
            inverse(d, e)
    for copy in iq:
        copy.wait_recv()

    def make_theta(j, carry):
        src = src_s[j]
        out = jnp.dot(blk[src, pl.ds(0, orb), :], inv_all[src], preferred_element_type=f32)
        theta[j] = out.astype(bf16).astype(f32).reshape(cols, tb, nel)
        return carry

    lax.fori_loop(0, walk_all, make_theta, 0)
    for k in range(group):
        picked_ref[k] = blk[src_s[k * ng + x], pl.ds(0, orb), :]

    def score_tile(i, carry):
        tile = proj[i].astype(f32)
        column = col_s[i]

        def one(w, inner):
            part = (tile * theta[w, column]).reshape(tb // 8, 8, nel)
            part = jnp.sum(part, axis=0)
            total = part[:, :128]
            for n in range(128, nel, 128):
                total = total + part[:, n : n + 128]
            scores[w, pl.ds(i, 1), :] = jnp.sum(total, axis=0, keepdims=True)
            return inner

        lax.fori_loop(0, walk_all, one, 0, unroll=4)
        return carry

    def forward(d):
        tz[d - 1].wait_recv()
        tile_x(d)

    cuts = [slots * d // nr for d in range(nr + 1)]
    lax.fori_loop(cuts[0], cuts[nr // 2], score_tile, 0)
    lax.fori_loop(cuts[nr // 2], cuts[nr], score_tile, 0)

    exact = lax.Precision.HIGHEST
    ones = jnp.ones((8, 128), f32)
    for w in range(walk_all):
        row = lax.dot_general(
            ones, scores[w], (((1,), (1,)), ((), ())), preferred_element_type=f32, precision=exact
        )
        score[pl.ds(w, 1), :] = row[:1]
    lane = lax.broadcasted_iota(jnp.int32, (walk_all, slots), 1)
    sc = jnp.where(lane < count_s[0], score[...], 0.0)
    vec_lane = meta_ref[0:1, :]
    hot = (
        lax.broadcasted_iota(jnp.int32, (vec, slots), 0) == vec_lane[:, :slots]
    ).astype(f32)
    bias_in[c] = lax.dot_general(
        sc, hot, (((1,), (1,)), ((), ())), preferred_element_type=f32, precision=exact
    )
    copies = []
    for e in range(1, nc):
        at = bias_in.at[c]
        copy = remote(at, at, b_s.at[e - 1], b_r.at[e - 1], c_peer(e))
        copy.start()
        copies.append(copy)
    for copy in copies:
        copy.wait()
    force = bias_in[0]
    for e in range(1, nc):
        force = force + bias_in[e]
    force_ref[...] = force
    field = (noise_ref[...] - SQRT_TAU * force).astype(bf16)
    lane2 = lax.broadcasted_iota(jnp.int32, (vec, 2 * slots), 1)
    mine = lane2 // slots == a % 2
    fits = (lane2 % slots < count_s[0]) & mine
    hot2 = jnp.where(
        fits & (lax.broadcasted_iota(jnp.int32, (vec, 2 * slots), 0) == vec_lane), 1.0, 0.0
    ).astype(bf16)
    places = jnp.where(mine[:8], meta_ref[1:2, :].astype(f32), 0.0)
    pad = sent.shape[1] - 8
    for g in range(ng):
        pick = lax.broadcasted_iota(jnp.int32, (pad, walk_all), 1) == (
            lax.broadcasted_iota(jnp.int32, (pad, walk_all), 0) * ng + g
        )
        rows = jnp.dot(pick.astype(f32).astype(bf16), field, preferred_element_type=f32).astype(bf16)
        coeff = jnp.dot(rows, hot2, preferred_element_type=f32)
        sent[g] = jnp.concatenate([coeff, places], axis=0).astype(bf16)
    copies = []
    for f in range(1, nw):
        copy = remote(
            sent.at[((a + f) % nw) % ng], got.at[a], c_s.at[f - 1], c_r.at[f - 1], w_peer(f)
        )
        copy.start()
        copies.append(copy)
    got[a] = sent[x]
    for d in range(1, nr):
        forward(d)
    for copy in copies:
        copy.wait()
    for p in range(nw // 2):
        coef_ref[p] = got[2 * p].astype(f32) + got[2 * p + 1].astype(f32)
    for copy in wz + tz + iq + list(wx.values()):
        copy.wait_send()
    own.wait()
    for copy in tx.values():
        copy.wait()


def gather(row, col, count, sources, walkers, inv, trial, tiles, cut, noise, meta, nr, ng, nc):
    f32 = jnp.float32
    bf16 = jnp.bfloat16
    nw = nr * ng
    orb, nel = walkers.shape
    slots, tb, _ = tiles.shape
    walk_all, vec = noise.shape
    group = walk_all // ng
    cols = orb // tb
    q = nel // nc
    pad = (group + 7) // 8 * 8
    j = tb // nr
    dma = pltpu.SemaphoreType.DMA
    vmem = pl.BlockSpec(memory_space=pltpu.VMEM)
    smem = pl.BlockSpec(memory_space=pltpu.SMEM)
    hbm = pl.BlockSpec(memory_space=pl.ANY)
    return pl.pallas_call(
        functools.partial(gather_kernel, nr, ng, nc),
        out_shape=(
            jax.ShapeDtypeStruct((walk_all, vec), f32),
            jax.ShapeDtypeStruct((nw // 2, pad + 8, 2 * slots), f32),
            jax.ShapeDtypeStruct((group, orb, nel), bf16),
            jax.ShapeDtypeStruct((j, nw * slots, tb), bf16),
        ),
        in_specs=[smem] * 4 + [vmem] * 4 + [hbm] + [vmem] * 2,
        out_specs=(vmem, vmem, vmem, hbm),
        scratch_shapes=[
            pltpu.VMEM((nw, orb + q, nel), bf16),
            pltpu.VMEM((nw, nel, nel), bf16),
            pltpu.VMEM((slots, tb, nel), bf16),
            pltpu.VMEM((walk_all, cols, tb, nel), f32),
            pltpu.VMEM((walk_all, slots, 128), f32),
            pltpu.VMEM((walk_all, slots), f32),
            pltpu.VMEM((nc, walk_all, vec), f32),
            pltpu.VMEM((ng, pad + 8, 2 * slots), bf16),
            pltpu.VMEM((nw, pad + 8, 2 * slots), bf16),
            dma((nr - 1,)),
            dma((nr - 1,)),
            dma((ng - 1, nr)),
            dma((ng - 1, nr)),
            dma((nr, ng, nc - 1)),
            dma((nr, ng, nc - 1)),
            dma((nr - 1,)),
            dma((nr - 1,)),
            dma((ng - 1, nr)),
            dma((ng - 1, nr)),
            dma,
            dma((nc - 1,)),
            dma((nc - 1,)),
            dma((nw - 1,)),
            dma((nw - 1,)),
        ],
        compiler_params=pltpu.CompilerParams(
            collective_id=1, has_side_effects=True, vmem_limit_bytes=VMEM_LIMIT
        ),
    )(row, col, count, sources, walkers, inv, trial, tiles, cut, noise, meta)


def series_kernel(
    nr,
    ng,
    nc,
    coef_ref,
    picked_ref,
    tin_ref,
    out_ref,
    wts,
    op32,
    op,
    term,
    total,
    own,
    c_send,
    c_recv,
    y_send,
    y_recv,
    fin,
    cs,
    cr,
    ys,
    yr,
    zs,
    zr,
    fs,
    fr,
):
    f32 = jnp.float32
    bf16 = jnp.bfloat16
    a = lax.axis_index("wide")
    c = lax.axis_index("chol")
    z = a // ng
    x = a % ng
    core = c % 2
    y = c // 2
    ny = nc // 2
    group, orb, nel = picked_ref.shape
    j_all, depth, tb = tin_ref.shape
    cols = orb // tb
    rows = op.shape[1]
    rblocks = rows // j_all
    piece = rows // nc
    half = rows // 2
    places = cols * rblocks
    pairs = coef_ref.shape[0]
    pad = coef_ref.shape[1] - 8
    items = TAYLOR * group

    def z_dev(to):
        return (to * ng + x, c)

    def c_dev(to):
        return (a, to)

    wait_all = meet(
        [z_dev((z + d) % nr) for d in range(1, nr)]
        + [c_dev(y * 2 + 1 - core)]
        + [c_dev(((y + e) % ny) * 2 + core) for e in range(1, ny)]
    )

    def lanes(row):
        return jnp.concatenate([coef_ref[p, row : row + 1, :] for p in range(pairs)], axis=1)

    spot = lanes(pad).astype(jnp.int32)
    hit = lax.broadcasted_iota(jnp.int32, (places, depth), 0) == spot
    for w in range(group):
        wts[pl.ds(w * places, places), :] = jnp.where(hit, lanes(w), 0.0).astype(bf16)
        term[0, w] = picked_ref[w].reshape(cols, nr, j_all, nel)
        total[w] = term[0, w, :, z].astype(f32).reshape(piece, nel)

    def build(j, carry):
        out = jnp.dot(wts[...], tin_ref[j], preferred_element_type=f32)
        for w in range(group):
            for col in range(cols):
                top = w * places + col * rblocks
                op32[w, col, pl.ds(j, rblocks, stride=j_all), :] = out[top : top + rblocks]
        return carry

    lax.fori_loop(0, j_all, build, 0)
    for w in range(group):
        for col in range(cols):
            op[w, :, pl.ds(col * tb, tb)] = op32[w, col].astype(bf16)
    wait_all()

    core_copy = {}
    y_copy = {}
    z_copy = {}

    def multiply(t):
        k, w = divmod(t, group)
        if k:
            for copy in z_copy[k, w]:
                copy.wait_recv()
        right = term[k, w].reshape(orb, nel)
        there = pl.ds(pl.multiple_of((1 - core) * half, half), half)
        here = pl.ds(pl.multiple_of(core * half, half), half)
        c_send[t] = jnp.dot(op[w, there, :], right, preferred_element_type=f32).astype(bf16)
        core_copy[t] = remote(
            c_send.at[t], c_recv.at[t], cs.at[t], cr.at[t], c_dev(y * 2 + 1 - core)
        )
        core_copy[t].start()
        own[t % 4] = jnp.dot(op[w, here, :], right, preferred_element_type=f32)

    def add_core(t):
        core_copy[t].wait_recv()
        for e in range(1, ny):
            to = (y + e) % ny
            at = pl.ds(pl.multiple_of(to * piece, piece), piece)
            y_send[t, e - 1] = (own[t % 4, at, :] + c_recv[t, at, :].astype(f32)).astype(bf16)
            y_copy[t, e] = remote(
                y_send.at[t, e - 1], y_recv.at[t, e - 1], ys.at[t, e - 1], yr.at[t, e - 1], c_dev(to * 2 + core)
            )
            y_copy[t, e].start()

    def finish(t):
        k, w = divmod(t, group)
        at = pl.ds(pl.multiple_of(y * piece, piece), piece)
        value = own[t % 4, at, :] + c_recv[t, at, :].astype(f32)
        for e in range(1, ny):
            y_copy[t, e].wait_recv()
            value = value + y_recv[t, e - 1].astype(f32)
        new = (SQRT_TAU / (k + 1) * value).astype(bf16)
        added = total[w] + new.astype(f32)
        if k < TAYLOR - 1:
            total[w] = added
            mine = term.at[k + 1, w, :, z]
            term[k + 1, w, :, z] = new.reshape(cols, j_all, nel)
            z_copy[k + 1, w] = []
            for d in range(1, nr):
                copy = remote(
                    mine, mine, zs.at[k, w, d - 1], zr.at[k, w, d - 1], z_dev((z + d) % nr)
                )
                copy.start()
                z_copy[k + 1, w].append(copy)
            return
        fin[w] = added.astype(bf16).reshape(cols, j_all, nel)

        @pl.when(z == w)
        def _():
            out_ref[:, z] = fin[w]

        @pl.when(z != w)
        def _():
            remote(fin.at[w], out_ref.at[:, z], fs.at[w], fr.at[z], z_dev(w)).start()

    for t in range(items + 2):
        if t < items:
            multiply(t)
        if 0 <= t - 1 < items:
            add_core(t - 1)
        if 0 <= t - 2 < items:
            finish(t - 2)
    for w in range(group):

        @pl.when(z != w)
        def _():
            copy = remote(fin.at[w], out_ref.at[:, w], fs.at[w], fr.at[w], z_dev(w))
            copy.wait_send()
            copy.wait_recv()

    for copy in list(core_copy.values()) + list(y_copy.values()):
        copy.wait_send()
    for copies in z_copy.values():
        for copy in copies:
            copy.wait_send()


def series(coef, picked, tin, rblocks, nr, ng, nc):
    f32 = jnp.float32
    bf16 = jnp.bfloat16
    group, orb, nel = picked.shape
    j, depth, tb = tin.shape
    cols = orb // tb
    rows = rblocks * j
    piece = rows // nc
    ny = nc // 2
    more = max(ny - 1, 1)
    items = TAYLOR * group
    dma = pltpu.SemaphoreType.DMA
    vmem = pl.BlockSpec(memory_space=pltpu.VMEM)
    return pl.pallas_call(
        functools.partial(series_kernel, nr, ng, nc),
        out_shape=jax.ShapeDtypeStruct((cols, nr, j, nel), bf16),
        in_specs=[vmem] * 3,
        out_specs=vmem,
        scratch_shapes=[
            pltpu.VMEM((group * cols * rblocks, depth), bf16),
            pltpu.VMEM((group, cols, rows, tb), f32),
            pltpu.VMEM((group, rows, orb), bf16),
            pltpu.VMEM((TAYLOR, group, cols, nr, j, nel), bf16),
            pltpu.VMEM((group, piece, nel), f32),
            pltpu.VMEM((4, rows // 2, nel), f32),
            pltpu.VMEM((items, rows // 2, nel), bf16),
            pltpu.VMEM((items, rows // 2, nel), bf16),
            pltpu.VMEM((items, more, piece, nel), bf16),
            pltpu.VMEM((items, more, piece, nel), bf16),
            pltpu.VMEM((group, cols, j, nel), bf16),
            dma((items,)),
            dma((items,)),
            dma((items, more)),
            dma((items, more)),
            dma((TAYLOR - 1, group, nr - 1)),
            dma((TAYLOR - 1, group, nr - 1)),
            dma((group,)),
            dma((group,)),
        ],
        compiler_params=pltpu.CompilerParams(
            collective_id=0, has_side_effects=True, vmem_limit_bytes=VMEM_LIMIT
        ),
    )(coef, picked, tin)


def body(
    walkers,
    intersection_inv,
    trial_state,
    chol_tiles,
    tile_vector,
    tile_row,
    tile_col,
    tile_count,
    sources,
    aux_noise,
):
    _, orb, nel = walkers.shape
    slots, tb, _ = chol_tiles.shape
    rblocks = trial_state.shape[0] // tb
    cols = orb // tb
    wide = lax.axis_size("wide")
    nc = lax.axis_size("chol")
    nr, ng = split_wide(wide, tb)
    block = tile_row // cols
    spot = ((block % 2) * (nc // 2) + block // 2) * cols + tile_row % cols
    place = tile_col * rblocks + spot
    meta = jnp.stack([jnp.tile(tile_vector, 2), jnp.tile(place, 2)])
    meta = jnp.concatenate([meta, jnp.zeros((6, 2 * slots), jnp.int32)])
    cut = jnp.transpose(chol_tiles.reshape(slots, nr, tb // nr, tb), (1, 2, 0, 3))
    force, coef, picked, tin = gather(
        tile_row,
        tile_col,
        tile_count,
        sources,
        walkers[0],
        intersection_inv[0],
        trial_state.reshape(rblocks, tb, nel),
        chol_tiles,
        cut,
        aux_noise,
        meta,
        nr,
        ng,
        nc,
    )
    out = series(coef, picked, tin, rblocks, nr, ng, nc)
    return (force, out.reshape(1, orb, nel))


def solution(mesh):
    return jax.shard_map(
        body,
        mesh=mesh,
        in_specs=(
            P("wide", "chol", None),
            P("wide", None, None),
            P(),
            P(("wide", "chol"), None, None),
            P(("wide", "chol")),
            P(("wide", "chol")),
            P(("wide", "chol")),
            P(("wide", "chol")),
            P(),
            P(None, "wide"),
        ),
        out_specs=(P(None, "wide"), P("wide", "chol", None)),
        check_vma=False,
    )
```

```python
import functools

import jax
import jax.numpy as jnp
from jax import lax
from jax.experimental import pallas as pl
from jax.experimental.pallas import tpu as pltpu
from jax.sharding import PartitionSpec as P

TAYLOR = 4


SQRT_TAU = 0.1
MESH = pl.DeviceIdType.MESH
VMEM_LIMIT = 60 * 1024 * 1024
CHUNK = 4
AHEAD = 2


def split_wide(wide, tile_size):
    parts = min(wide // 2, tile_size // 16)
    return parts, wide // parts


def remote(src, dst, send, recv, device):
    return pltpu.make_async_remote_copy(
        src_ref=src, dst_ref=dst, send_sem=send, recv_sem=recv, device_id=device, device_id_type=MESH
    )


def meet(peers):
    barrier = pltpu.get_barrier_semaphore()
    for peer in peers:
        pl.semaphore_signal(barrier, inc=1, device_id=peer, device_id_type=MESH)
    return lambda: pl.semaphore_wait(barrier, len(peers))


def step_kernel(
    nr,
    ng,
    nc,
    row_s,
    col_s,
    count_s,
    src_s,
    walk_ref,
    inv_ref,
    trial_ref,
    tiles_ref,
    cut_ref,
    noise_ref,
    vec_ref,
    place_ref,
    force_ref,
    out_ref,
    blk,
    inv_all,
    proj,
    theta,
    scores,
    score,
    bias_in,
    sent,
    got,
    tin,
    wts,
    op32,
    op,
    term,
    total,
    own,
    c_send,
    c_recv,
    y_send,
    y_recv,
    fin,
    wu_s,
    wu_r,
    wd_s,
    wd_r,
    wx_s,
    wx_r,
    iq_s,
    iq_r,
    tz_s,
    tz_r,
    tx_s,
    tx_r,
    own_s,
    b_s,
    b_r,
    g_s,
    g_r,
    cs,
    cr,
    ys,
    yr,
    zs,
    zr,
    fs,
    fr,
):
    f32 = jnp.float32
    bf16 = jnp.bfloat16
    nw = nr * ng
    ny = nc // 2
    a = lax.axis_index("wide")
    c = lax.axis_index("chol")
    z = a // ng
    x = a % ng
    core = c % 2
    y = c // 2
    orb, nel = walk_ref.shape
    q = nel // nc
    slots, tb, _ = tiles_ref.shape
    walk_all, vec = noise_ref.shape
    group = walk_all // ng
    cols = orb // tb
    j_all = tb // nr
    part = CHUNK
    chunks = j_all // part
    depth = nw * slots
    rows = op.shape[1]
    rblocks = rows // j_all
    piece = rows // nc
    half = rows // 2
    places = cols * rblocks
    pad = sent.shape[1] - 8
    items = TAYLOR * group

    def z_dev(to):
        return (to * ng + x, c)

    def x_dev(e):
        return (z * ng + (x + e) % ng, c)

    def c_dev(to):
        return (a, to)

    def c_peer(e):
        return (a, (c + e) % nc)

    def w_peer(f):
        return ((a + f) % nw, c)

    def slab(d, e):
        return ((z + nr - d) % nr) * ng + (x + ng - e) % ng

    ends = []

    def later(condition, action):
        ends.append((condition, action))

    wait_all = meet([w_peer(f) for f in range(1, nw)] + [c_peer(e) for e in range(1, nc)])
    q_at = pl.ds(pl.multiple_of(c * q, 16), q)
    blk[a, pl.ds(0, orb), :] = walk_ref[...]
    blk[a, pl.ds(orb, q), :] = inv_ref[q_at, :]
    wait_all()

    def has(s, side):
        return z - s >= 0 if side == 0 else z + s < nr

    def source(s, side):
        return z - s if side == 0 else z + s

    def link(s, side):
        at = blk.at[source(s, side) * ng + x]
        send, recv = (wu_s, wu_r) if side == 0 else (wd_s, wd_r)
        return lambda i: remote(
            at, at, send.at[i], recv.at[i], z_dev((z + 1) % nr if side == 0 else (z + nr - 1) % nr)
        )

    def pass_on(s, side):
        ahead = z + 1 < nr if side == 0 else z - 1 >= 0

        @pl.when(has(s, side) & ahead)
        def _():
            link(s, side)(s).start()

    def passed(s, side):
        ahead = z + 1 < nr if side == 0 else z - 1 >= 0

        @pl.when(has(s, side) & ahead)
        def _():
            link(s, side)(s).wait_send()

    def walk_x(zz, e):
        at = blk.at[zz * ng + x]
        return remote(at, at, wx_s.at[e - 1, zz], wx_r.at[e - 1, zz], x_dev(e))

    def inverse_copy(s, f):
        return remote(
            blk.at[s, pl.ds(orb, q)],
            inv_all.at[s, q_at],
            iq_s.at[s, f - 1],
            iq_r.at[s, f - 1],
            c_peer(f),
        )

    def inverse(s):
        inv_all[s, q_at, :] = blk[s, pl.ds(orb, q), :]
        for f in range(1, nc):
            inverse_copy(s, f).start()

    def arrive(s, side):
        @pl.when(has(s, side))
        def _():
            link(s, side)(s - 1).wait_recv()

        if s < nr - 1:
            pass_on(s, side)

        @pl.when(has(s, side))
        def _():
            zz = source(s, side)
            for e in range(1, ng):
                walk_x(zz, e).start()
            inverse(zz * ng + x)

    def tile_at(k, s):
        return tin.at[pl.ds(k * part, part), pl.ds(pl.multiple_of(s * slots, slots), slots), :]

    def cut_at(k, to):
        return cut_ref.at[to, pl.ds(k * part, part)]

    tz = {}
    tx = {}

    def tile_z(k):
        for d in sorted(range(1, nr), key=lambda d: abs(d - nr / 2)):
            tz[k, d] = remote(
                cut_at(k, (z + d) % nr), tile_at(k, a), tz_s.at[k, d - 1], tz_r.at[k, d - 1], z_dev((z + d) % nr)
            )
            tz[k, d].start()

    def tile_x(k, d):
        at = tile_at(k, slab(d, 0))
        for e in range(1, ng):
            tx[k, d, e] = remote(
                cut_at(k, z) if d == 0 else at, at, tx_s.at[e - 1, k, d], tx_r.at[e - 1, k, d], x_dev(e)
            )
            tx[k, d, e].start()

    todo = list(range(chunks))

    def tile_event():
        if not todo:
            return
        k = todo.pop(0)
        for d in range(1, nr):
            tz[k, d].wait_send()
        if k + AHEAD < chunks:
            tile_z(k + AHEAD)
        for d in sorted(range(1, nr), key=lambda d: -abs(d - nr / 2)):
            tz[k, d].wait_recv()
            tile_x(k, d)

    pass_on(0, 0)
    pass_on(0, 1)
    for e in range(1, ng):
        walk_x(z, e).start()
    for k in range(chunks):
        tile_x(k, 0)
    own_copy = pltpu.make_async_copy(
        cut_ref.at[z], tin.at[:, pl.ds(pl.multiple_of(a * slots, slots), slots), :], own_s
    )
    own_copy.start()
    inverse(a)

    def project(i, carry):
        out = lax.dot_general(
            tiles_ref[i], trial_ref[row_s[i]], (((0,), (0,)), ((), ())), preferred_element_type=f32
        )
        proj[i] = out.astype(bf16)
        return carry

    cuts = [slots * d // nr for d in range(nr + 1)]
    for s in range(1, nr):
        lax.fori_loop(cuts[s - 1], cuts[s], project, 0)
        arrive(s, 0)
        arrive(s, 1)
        if s == min(2, nr - 1):
            for k in range(min(AHEAD, chunks)):
                tile_z(k)
    lax.fori_loop(cuts[nr - 1], cuts[nr], project, 0)
    tile_event()
    for e in range(1, ng):
        for zz in range(nr):
            walk_x(zz, e).wait_recv()
            inverse(zz * ng + (x + ng - e) % ng)
    for s in range(nw):
        for f in range(1, nc):
            inverse_copy(s, f).wait_recv()

    def make_theta(j, carry):
        src = src_s[j]
        out = jnp.dot(blk[src, pl.ds(0, orb), :], inv_all[src], preferred_element_type=f32)
        theta[j] = out.astype(bf16).astype(f32).reshape(cols, tb, nel)
        return carry

    lax.fori_loop(0, walk_all, make_theta, 0)
    tile_event()

    def score_tile(i, carry):
        tile = proj[i].astype(f32)
        column = col_s[i]

        def one(w, inner):
            value = (tile * theta[w, column]).reshape(tb // 8, 8, nel)
            value = jnp.sum(value, axis=0)
            lanes = value[:, :128]
            for n in range(128, nel, 128):
                lanes = lanes + value[:, n : n + 128]
            scores[w, pl.ds(i, 1), :] = jnp.sum(lanes, axis=0, keepdims=True)
            return inner

        lax.fori_loop(0, walk_all, one, 0, unroll=4)
        return carry

    lax.fori_loop(0, slots // 2, score_tile, 0)
    tile_event()
    lax.fori_loop(slots // 2, slots, score_tile, 0)

    exact = lax.Precision.HIGHEST
    ones = jnp.ones((8, 128), f32)
    for w in range(walk_all):
        row = lax.dot_general(
            ones, scores[w], (((1,), (1,)), ((), ())), preferred_element_type=f32, precision=exact
        )
        score[pl.ds(w, 1), :] = row[:1]
    lane = lax.broadcasted_iota(jnp.int32, (walk_all, slots), 1)
    sc = jnp.where(lane < count_s[0], score[...], 0.0)
    hot = (lax.broadcasted_iota(jnp.int32, (vec, slots), 0) == vec_ref[...]).astype(f32)
    bias_in[c] = lax.dot_general(
        sc, hot, (((1,), (1,)), ((), ())), preferred_element_type=f32, precision=exact
    )
    bias_copies = []
    for e in range(1, nc):
        at = bias_in.at[c]
        copy = remote(at, at, b_s.at[e - 1], b_r.at[e - 1], c_peer(e))
        copy.start()
        bias_copies.append(copy)
    for k in range(group):
        first = blk[src_s[k * ng + x], pl.ds(0, orb), :]
        term[0, k] = first.reshape(cols, nr, j_all, nel)
        total[k] = term[0, k, :, z].astype(f32).reshape(piece, nel)
    tile_event()
    for copy in bias_copies:
        copy.wait_recv()
    force = bias_in[0]
    for e in range(1, nc):
        force = force + bias_in[e]
    force_ref[...] = force
    field = (noise_ref[...] - SQRT_TAU * force).astype(bf16)
    lane2 = lax.broadcasted_iota(jnp.int32, (vec, 2 * slots), 1)
    mine = lane2 // slots == a % 2
    fits = (lane2 % slots < count_s[0]) & mine
    vec2 = jnp.concatenate([vec_ref[...]] * 2, axis=1)
    hot2 = jnp.where(
        fits & (lax.broadcasted_iota(jnp.int32, (vec, 2 * slots), 0) == vec2), 1.0, 0.0
    ).astype(bf16)
    place2 = jnp.concatenate([place_ref[...]] * 2, axis=1)
    spots = jnp.where(mine[:8], place2.astype(f32), 0.0)
    for g in range(ng):
        pick = lax.broadcasted_iota(jnp.int32, (pad, walk_all), 1) == (
            lax.broadcasted_iota(jnp.int32, (pad, walk_all), 0) * ng + g
        )
        fields = jnp.dot(pick.astype(f32).astype(bf16), field, preferred_element_type=f32)
        coeff = jnp.dot(fields.astype(bf16), hot2, preferred_element_type=f32)
        sent[g] = jnp.concatenate([coeff, spots], axis=0).astype(bf16)
    sent_copies = []
    for f in range(1, nw):
        copy = remote(
            sent.at[((a + f) % nw) % ng], got.at[a], g_s.at[f - 1], g_r.at[f - 1], w_peer(f)
        )
        copy.start()
        sent_copies.append(copy)
    got[a] = sent[x]
    tile_event()
    for copy in sent_copies:
        copy.wait_recv()

    def lanes(at):
        return jnp.concatenate(
            [got[2 * p].astype(f32)[at : at + 1] + got[2 * p + 1].astype(f32)[at : at + 1] for p in range(nw // 2)],
            axis=1,
        )

    hit = lax.broadcasted_iota(jnp.int32, (places, depth), 0) == lanes(pad).astype(jnp.int32)
    for w in range(group):
        wts[pl.ds(w * places, places), :] = jnp.where(hit, lanes(w), 0.0).astype(bf16)

    def build(j, carry):
        out = jnp.dot(wts[...], tin[j], preferred_element_type=f32)
        for w in range(group):
            for col in range(cols):
                top = w * places + col * rblocks
                op32[w, col, pl.ds(j, rblocks, stride=j_all), :] = out[top : top + rblocks]
        return carry

    tile_event()
    own_copy.wait()
    for k in range(chunks):
        if k == chunks - part:
            while todo:
                tile_event()
        for d in range(nr):
            for e in range(1, ng):
                tx[k, d, e].wait_recv()
        lax.fori_loop(k * part, (k + 1) * part, build, 0)
        if k % 2 == 1:
            tile_event()
    for w in range(group):
        for col in range(cols):
            op[w, :, pl.ds(col * tb, tb)] = op32[w, col].astype(bf16)

    core_copy = {}
    y_copy = {}
    z_copy = {}

    def multiply(t):
        k, w = divmod(t, group)
        if k:
            for d in range(1, nr):
                z_wait(t - group, d)
        right = term[k, w].reshape(orb, nel)
        there = pl.ds(pl.multiple_of((1 - core) * half, half), half)
        here = pl.ds(pl.multiple_of(core * half, half), half)
        c_send[t] = jnp.dot(op[w, there, :], right, preferred_element_type=f32).astype(bf16)
        core_copy[t] = remote(
            c_send.at[t], c_recv.at[t], cs.at[t], cr.at[t], c_dev(y * 2 + 1 - core)
        )
        core_copy[t].start()
        own[t % 4] = jnp.dot(op[w, here, :], right, preferred_element_type=f32)

    def add_core(t):
        core_copy[t].wait_recv()
        for e in range(1, ny):
            to = (y + e) % ny
            at = pl.ds(pl.multiple_of(to * piece, piece), piece)
            y_send[t, e - 1] = (own[t % 4, at, :] + c_recv[t, at, :].astype(f32)).astype(bf16)
            y_copy[t, e] = remote(
                y_send.at[t, e - 1], y_recv.at[t, e - 1], ys.at[t, e - 1], yr.at[t, e - 1], c_dev(to * 2 + core)
            )
            y_copy[t, e].start()

    def relay(t):
        k, w = divmod(t, group)
        if k == TAYLOR - 1 or nr < 3:
            return
        for at_z, from_z, d in ((nr - 2, 0, nr - 2), (1, nr - 1, 2)):

            @pl.when(z == at_z)
            def _():
                z_send(t, d, from_z).wait_recv()
                relay_copy(t, from_z).start()

            later(z == at_z, lambda from_z=from_z: relay_copy(t, from_z).wait_send())

    def relay_copy(t, from_z):
        k, w = divmod(t, group)
        at = term.at[k + 1, w, :, from_z]
        d = nr - 1 if from_z == 0 else 1
        return remote(at, at, zs.at[k, w, nr - 1], zr.at[k, w, d - 1], z_dev(nr - 1 - from_z))

    def z_send(t, d, from_z):
        k, w = divmod(t, group)
        at = term.at[k + 1, w, :, from_z]
        return remote(at, at, zs.at[k, w, d - 1], zr.at[k, w, d - 1], z_dev((from_z + d) % nr))

    def far(d, sender):
        if nr < 3:
            return False
        if d == nr - 1:
            return sender == 0
        if d == 1:
            return sender == nr - 1
        return False

    def z_wait(t, d):
        here = (z + nr - d) % nr
        taken = False
        if nr >= 3:
            if d == nr - 2:
                taken = z == nr - 2
            if d == 2:
                taken = (z == 1) if taken is False else taken | (z == 1)
        if taken is False:
            z_send(t, d, here).wait_recv()
        else:

            @pl.when(jnp.logical_not(taken))
            def _():
                z_send(t, d, here).wait_recv()

    def finish(t):
        k, w = divmod(t, group)
        at = pl.ds(pl.multiple_of(y * piece, piece), piece)
        value = own[t % 4, at, :] + c_recv[t, at, :].astype(f32)
        for e in range(1, ny):
            y_copy[t, e].wait_recv()
            value = value + y_recv[t, e - 1].astype(f32)
        new = (SQRT_TAU / (k + 1) * value).astype(bf16)
        added = total[w] + new.astype(f32)
        if k < TAYLOR - 1:
            total[w] = added
            term[k + 1, w, :, z] = new.reshape(cols, j_all, nel)
            for d in range(1, nr):
                skip = far(d, z)
                if skip is False:
                    z_send(t, d, z).start()
                    later(None, lambda d=d: z_send(t, d, z).wait_send())
                else:

                    @pl.when(jnp.logical_not(skip))
                    def _():
                        z_send(t, d, z).start()

                    later(jnp.logical_not(skip), lambda d=d: z_send(t, d, z).wait_send())
            return
        fin[w] = added.astype(bf16).reshape(cols, j_all, nel)

        @pl.when(z == w)
        def _():
            out_ref[:, z] = fin[w]

        @pl.when(z != w)
        def _():
            remote(fin.at[w], out_ref.at[:, z], fs.at[w], fr.at[z], z_dev(w)).start()

    for t in range(items + 2):
        if 0 <= t - 3 < items:
            relay(t - 3)
        if t < items:
            multiply(t)
        if 0 <= t - 1 < items:
            add_core(t - 1)
        if 0 <= t - 2 < items:
            finish(t - 2)
    for w in range(group):

        @pl.when(z != w)
        def _():
            copy = remote(fin.at[w], out_ref.at[:, w], fs.at[w], fr.at[w], z_dev(w))
            copy.wait_send()
            copy.wait_recv()

    for s in range(nr - 1):
        passed(s, 0)
        passed(s, 1)
    for zz in range(nr):
        for e in range(1, ng):
            walk_x(zz, e).wait_send()
    for s in range(nw):
        for f in range(1, nc):
            inverse_copy(s, f).wait_send()
    for copy in list(tx.values()) + bias_copies + sent_copies:
        copy.wait_send()
    for copy in list(core_copy.values()) + list(y_copy.values()):
        copy.wait_send()
    for condition, action in ends:
        if condition is None:
            action()
        else:
            pl.when(condition)(action)


def step(row, col, count, sources, walkers, inv, trial, tiles, cut, noise, vector, place, nr, ng, nc):
    f32 = jnp.float32
    bf16 = jnp.bfloat16
    nw = nr * ng
    orb, nel = walkers.shape
    slots, tb, _ = tiles.shape
    walk_all, vec = noise.shape
    group = walk_all // ng
    cols = orb // tb
    q = nel // nc
    pad = (group + 7) // 8 * 8
    j = tb // nr
    chunks = j // CHUNK
    rblocks = trial.shape[0]
    rows = rblocks * j
    piece = rows // nc
    more = max(nc // 2 - 1, 1)
    items = TAYLOR * group
    dma = pltpu.SemaphoreType.DMA
    vmem = pl.BlockSpec(memory_space=pltpu.VMEM)
    smem = pl.BlockSpec(memory_space=pltpu.SMEM)
    hbm = pl.BlockSpec(memory_space=pl.ANY)

    def both(*shape):
        return [dma(shape), dma(shape)]

    return pl.pallas_call(
        functools.partial(step_kernel, nr, ng, nc),
        out_shape=(
            jax.ShapeDtypeStruct((walk_all, vec), f32),
            jax.ShapeDtypeStruct((cols, nr, j, nel), bf16),
        ),
        in_specs=[smem] * 4 + [vmem] * 4 + [hbm] + [vmem] * 3,
        out_specs=(vmem, vmem),
        scratch_shapes=[
            pltpu.VMEM((nw, orb + q, nel), bf16),
            pltpu.VMEM((nw, nel, nel), bf16),
            pltpu.VMEM((slots, tb, nel), bf16),
            pltpu.VMEM((walk_all, cols, tb, nel), f32),
            pltpu.VMEM((walk_all, slots, 128), f32),
            pltpu.VMEM((walk_all, slots), f32),
            pltpu.VMEM((nc, walk_all, vec), f32),
            pltpu.VMEM((ng, pad + 8, 2 * slots), bf16),
            pltpu.VMEM((nw, pad + 8, 2 * slots), bf16),
            pltpu.VMEM((j, nw * slots, tb), bf16),
            pltpu.VMEM((group * cols * rblocks, nw * slots), bf16),
            pltpu.VMEM((group, cols, rows, tb), f32),
            pltpu.VMEM((group, rows, orb), bf16),
            pltpu.VMEM((TAYLOR, group, cols, nr, j, nel), bf16),
            pltpu.VMEM((group, piece, nel), f32),
            pltpu.VMEM((4, rows // 2, nel), f32),
            pltpu.VMEM((items, rows // 2, nel), bf16),
            pltpu.VMEM((items, rows // 2, nel), bf16),
            pltpu.VMEM((items, more, piece, nel), bf16),
            pltpu.VMEM((items, more, piece, nel), bf16),
            pltpu.VMEM((group, cols, j, nel), bf16),
        ]
        + both(nr - 1)
        + both(nr - 1)
        + both(ng - 1, nr)
        + both(nw, nc - 1)
        + both(chunks, nr - 1)
        + both(ng - 1, chunks, nr)
        + [dma]
        + both(nc - 1)
        + both(nw - 1)
        + both(items)
        + both(items, more)
        + both(TAYLOR - 1, group, nr)
        + both(group),
        compiler_params=pltpu.CompilerParams(
            collective_id=0, has_side_effects=True, vmem_limit_bytes=VMEM_LIMIT
        ),
    )(row, col, count, sources, walkers, inv, trial, tiles, cut, noise, vector, place)


def body(
    walkers,
    intersection_inv,
    trial_state,
    chol_tiles,
    tile_vector,
    tile_row,
    tile_col,
    tile_count,
    sources,
    aux_noise,
):
    _, orb, nel = walkers.shape
    slots, tb, _ = chol_tiles.shape
    rblocks = trial_state.shape[0] // tb
    cols = orb // tb
    wide = lax.axis_size("wide")
    nc = lax.axis_size("chol")
    nr, ng = split_wide(wide, tb)
    block = tile_row // cols
    spot = ((block % 2) * (nc // 2) + block // 2) * cols + tile_row % cols
    place = tile_col * rblocks + spot
    cut = jnp.transpose(chol_tiles.reshape(slots, nr, tb // nr, tb), (1, 2, 0, 3))
    force, out = step(
        tile_row,
        tile_col,
        tile_count,
        sources,
        walkers[0],
        intersection_inv[0],
        trial_state.reshape(rblocks, tb, nel),
        chol_tiles,
        cut,
        aux_noise,
        tile_vector.reshape(1, slots),
        place.reshape(1, slots),
        nr,
        ng,
        nc,
    )
    return (force, out.reshape(1, orb, nel))


def solution(mesh):
    return jax.shard_map(
        body,
        mesh=mesh,
        in_specs=(
            P("wide", "chol", None),
            P("wide", None, None),
            P(),
            P(("wide", "chol"), None, None),
            P(("wide", "chol")),
            P(("wide", "chol")),
            P(("wide", "chol")),
            P(("wide", "chol")),
            P(),
            P(None, "wide"),
        ),
        out_specs=(P(None, "wide"), P("wide", "chol", None)),
        check_vma=False,
    )
```

```python
import functools

import jax
import jax.numpy as jnp
from jax import lax
from jax.experimental import pallas as pl
from jax.experimental.pallas import tpu as pltpu
from jax.sharding import PartitionSpec as P

TAYLOR = 4


SQRT_TAU = 0.1
MESH = pl.DeviceIdType.MESH
VMEM_LIMIT = 60 * 1024 * 1024
CHUNK = 4
OWN_FIRST = 2
EVENTS = (1, 0, 1, 0, 1, 0, 1)
BEFORE = 6
ROWS = 16
PARTS = 2
LAG_CORE = 1
LAG_Y = 2
LAG_RELAY = 3


def split_wide(wide, tile_size):
    parts = min(wide // 2, tile_size // 16)
    return parts, wide // parts


def remote(src, dst, send, recv, device):
    return pltpu.make_async_remote_copy(
        src_ref=src, dst_ref=dst, send_sem=send, recv_sem=recv, device_id=device, device_id_type=MESH
    )


def meet(peers):
    barrier = pltpu.get_barrier_semaphore()
    for peer in peers:
        pl.semaphore_signal(barrier, inc=1, device_id=peer, device_id_type=MESH)
    return lambda: pl.semaphore_wait(barrier, len(peers))


def step_kernel(
    nr,
    ng,
    nc,
    row_s,
    col_s,
    count_s,
    src_s,
    walk_ref,
    inv_ref,
    trial_hbm,
    tiles_hbm,
    noise_ref,
    vec_ref,
    row_ref,
    col_ref,
    force_ref,
    out_ref,
    blk,
    inv_all,
    proj,
    theta,
    scores,
    bias_in,
    sent,
    got,
    tin,
    wts,
    op32,
    op,
    term,
    total,
    own,
    c_send,
    c_recv,
    y_send,
    y_recv,
    fin,
    trial_ref,
    tiles_ref,
    cut,
    load_s,
    wu_s,
    wu_r,
    wd_s,
    wd_r,
    wx_s,
    wx_r,
    iq_s,
    iq_r,
    tz_s,
    tz_r,
    tx_s,
    tx_r,
    own_s,
    b_s,
    b_r,
    g_s,
    g_r,
    cs,
    cr,
    ys,
    yr,
    zs,
    zr,
    fs,
    fr,
):
    f32 = jnp.float32
    bf16 = jnp.bfloat16
    nw = nr * ng
    ny = nc // 2
    a = lax.axis_index("wide")
    c = lax.axis_index("chol")
    z = a // ng
    x = a % ng
    core = c % 2
    y = c // 2
    orb, nel = walk_ref.shape
    q = nel // nc
    slots, tb, _ = tiles_ref.shape
    walk_all, vec = noise_ref.shape
    group = walk_all // ng
    cols = orb // tb
    j_all = tb // nr
    part = CHUNK
    chunks = j_all // part
    depth = nw * slots
    halves = j_all // ROWS
    rblocks = trial_ref.shape[0]
    rows = rblocks * ROWS
    piece = rows // nc
    half = rows // 2
    places = cols * rblocks
    pad = sent.shape[1] - 8

    def z_dev(to):
        return (to * ng + x, c)

    def x_dev(e):
        return (z * ng + (x + e) % ng, c)

    def c_dev(to):
        return (a, to)

    def c_peer(e):
        return (a, (c + e) % nc)

    def w_peer(f):
        return ((a + f) % nw, c)

    def slab(d, e):
        return ((z + nr - d) % nr) * ng + (x + ng - e) % ng

    ends = []

    def later(condition, action):
        ends.append((condition, action))

    q_at = pl.ds(pl.multiple_of(c * q, 16), q)
    loads = [
        pltpu.make_async_copy(src, dst, load_s.at[n])
        for n, (src, dst) in enumerate(
            (
                (walk_ref, blk.at[a, pl.ds(0, orb)]),
                (inv_ref.at[q_at], blk.at[a, pl.ds(orb, q)]),
                (tiles_hbm, tiles_ref),
                (trial_hbm, trial_ref),
            )
        )
    ]
    for load in loads:
        load.start()
    wait_all = meet([w_peer(f) for f in range(1, nw)] + [c_peer(e) for e in range(1, nc)])
    loads[0].wait()
    loads[1].wait()
    wait_all()

    def has(s, side):
        return z - s >= 0 if side == 0 else z + s < nr

    def source(s, side):
        return z - s if side == 0 else z + s

    span = (orb + q) // PARTS

    def link(s, side, h):
        at = blk.at[source(s, side) * ng + x, pl.ds(h * span, span)]
        send, recv = (wu_s, wu_r) if side == 0 else (wd_s, wd_r)
        return lambda i: remote(
            at, at, send.at[i, h], recv.at[i, h], z_dev((z + 1) % nr if side == 0 else (z + nr - 1) % nr)
        )

    def pass_on(s, side, h):
        ahead = z + 1 < nr if side == 0 else z - 1 >= 0

        @pl.when(has(s, side) & ahead)
        def _():
            link(s, side, h)(s).start()

    def passed(s, side):
        ahead = z + 1 < nr if side == 0 else z - 1 >= 0

        @pl.when(has(s, side) & ahead)
        def _():
            for h in range(PARTS):
                link(s, side, h)(s).wait_send()

    def walk_x(zz, e, h):
        at = blk.at[zz * ng + x, pl.ds(h * span, span)]
        return remote(at, at, wx_s.at[e - 1, zz, h], wx_r.at[e - 1, zz, h], x_dev(e))

    def inverse_copy(s, f):
        return remote(
            blk.at[s, pl.ds(orb, q)],
            inv_all.at[s, q_at],
            iq_s.at[s, f - 1],
            iq_r.at[s, f - 1],
            c_peer(f),
        )

    def inverse(s):
        inv_all[s, q_at, :] = blk[s, pl.ds(orb, q), :]
        for f in range(1, nc):
            inverse_copy(s, f).start()

    def arrive(s, side, h):
        @pl.when(has(s, side))
        def _():
            link(s, side, h)(s - 1).wait_recv()

        if s < nr - 1:
            pass_on(s, side, h)

        @pl.when(has(s, side))
        def _():
            zz = source(s, side)
            for e in range(1, ng):
                walk_x(zz, e, h).start()
            if h == PARTS - 1:
                inverse(zz * ng + x)

    def tile_at(k, s):
        return tin.at[pl.ds(k * part, part), pl.ds(pl.multiple_of(s * slots, slots), slots), :]

    def cut_at(k, to):
        return cut.at[pl.ds(to * j_all + k * part, part)]

    tz = {}
    tx = {}

    def tile_z(k):
        for d in sorted(range(1, nr), key=lambda d: abs(d - nr / 2)):
            tz[k, d] = remote(
                cut_at(k, (z + d) % nr), tile_at(k, a), tz_s.at[k, d - 1], tz_r.at[k, d - 1], z_dev((z + d) % nr)
            )
            tz[k, d].start()

    def tile_x(k, d):
        at = tile_at(k, slab(d, 0))
        for e in range(1, ng):
            tx[k, d, e] = remote(
                cut_at(k, z) if d == 0 else at, at, tx_s.at[e - 1, k, d], tx_r.at[e - 1, k, d], x_dev(e)
            )
            tx[k, d, e].start()

    todo = list(range(chunks))

    def tile_event():
        if not todo or (todo[0], 1) not in tz:
            return
        k = todo.pop(0)
        for d in sorted(range(1, nr), key=lambda d: -abs(d - nr / 2)):
            tz[k, d].wait_recv()
            tile_x(k, d)

    for h in reversed(range(PARTS)):
        pass_on(0, 0, h)
        pass_on(0, 1, h)
        for e in range(1, ng):
            walk_x(z, e, h).start()
    inverse(a)
    loads[2].wait()

    def spread(i, carry):
        op32[pl.ds(i, tb, stride=slots), :] = tiles_ref[i].astype(f32)
        return carry

    def collect(p, carry):
        cut[p] = op32[pl.ds(pl.multiple_of(p * slots, slots), slots), :].astype(bf16)
        return carry

    lax.fori_loop(0, slots, spread, 0, unroll=2)
    lax.fori_loop(0, tb, collect, 0, unroll=4)
    for k in range(chunks * OWN_FIRST // 8):
        tile_x(k, 0)
    own_copy = pltpu.make_async_copy(
        cut.at[pl.ds(z * j_all, j_all)], tin.at[:, pl.ds(pl.multiple_of(a * slots, slots), slots), :], own_s
    )
    own_copy.start()
    loads[3].wait()

    def project(i, carry):
        out = lax.dot_general(
            tiles_ref[i], trial_ref[row_s[i]], (((0,), (0,)), ((), ())), preferred_element_type=f32
        )
        proj[i] = out.astype(bf16)
        return carry

    cuts = [slots * d // nr for d in range(nr + 1)]
    for s in range(1, nr):
        lax.fori_loop(cuts[s - 1], cuts[s], project, 0)
        for h in reversed(range(PARTS)):
            arrive(s, 0, h)
            arrive(s, 1, h)
        if s == min(2, nr - 1):
            for k in range(chunks * 2 // 8):
                tile_z(k)
    lax.fori_loop(cuts[nr - 1], cuts[nr], project, 0)
    for k in range(chunks * OWN_FIRST // 8, chunks):
        tile_x(k, 0)
    for k in range(chunks * 2 // 8, chunks * BEFORE // 8):
        tile_z(k)
    for _ in range(EVENTS[0]):
        tile_event()
    for e in range(1, ng):
        for zz in range(nr):
            if zz == nr // 2:
                for _ in range(EVENTS[1]):
                    tile_event()
            for h in range(PARTS):
                walk_x(zz, e, h).wait_recv()
            inverse(zz * ng + (x + ng - e) % ng)
    for _ in range(EVENTS[2]):
        tile_event()
    for s in range(nw):
        for f in range(1, nc):
            inverse_copy(s, f).wait_recv()

    def make_theta(j, carry):
        src = src_s[j]
        out = jnp.dot(blk[src, pl.ds(0, orb), :], inv_all[src], preferred_element_type=f32)
        theta[j] = out.astype(bf16).astype(f32).reshape(cols, tb, nel)
        return carry

    lax.fori_loop(0, walk_all, make_theta, 0)
    for _ in range(EVENTS[3]):
        tile_event()

    def score_tile(i, carry):
        tile = proj[i].astype(f32)
        column = col_s[i]

        def one(w, inner):
            value = (tile * theta[w, column]).reshape(tb // 8, 8, nel)
            value = jnp.sum(value, axis=0)
            lanes = value[:, :128]
            for n in range(128, nel, 128):
                lanes = lanes + value[:, n : n + 128]
            scores[w, pl.ds(i, 1), :] = jnp.sum(lanes, axis=0, keepdims=True)
            return inner

        lax.fori_loop(0, walk_all, one, 0, unroll=4)
        return carry

    lax.fori_loop(0, slots // 2, score_tile, 0)
    for _ in range(EVENTS[4]):
        tile_event()
    lax.fori_loop(slots // 2, slots, score_tile, 0)

    ones = jnp.ones((walk_all, 128), bf16)
    across = (((1,), (1,)), ((), ()))

    def dot2(value, other, flip):
        high = value.astype(bf16)
        low = (value - high.astype(f32)).astype(bf16)
        return sum(
            lax.dot_general(*((other, v) if flip else (v, other)), across, preferred_element_type=f32)
            for v in (high, low)
        )

    each = dot2(scores[...].reshape(walk_all * slots, 128), ones, True)
    lane = lax.broadcasted_iota(jnp.int32, each.shape, 1)
    keep = (lane // slots == lax.broadcasted_iota(jnp.int32, each.shape, 0)) & (
        lane % slots < count_s[0]
    )
    vec2 = jnp.concatenate([vec_ref[...]] * 2, axis=1)
    hot = (lax.broadcasted_iota(jnp.int32, (vec, 2 * slots), 0) == vec2).astype(f32).astype(bf16)
    hot = jnp.concatenate([hot] * (walk_all // 2), axis=1)
    bias_in[c] = dot2(jnp.where(keep, each, 0.0), hot, False)
    bias_copies = []
    for e in range(1, nc):
        at = bias_in.at[c]
        copy = remote(at, at, b_s.at[e - 1], b_r.at[e - 1], c_peer(e))
        copy.start()
        bias_copies.append(copy)
    for k in range(group):
        first = blk[src_s[k * ng + x], pl.ds(0, orb), :]
        term[0, k] = first.reshape(cols, nr, halves, ROWS, nel)
        for h in range(halves):
            total[k, h] = term[0, k, :, z, h].astype(f32).reshape(piece, nel)
    for _ in range(EVENTS[5]):
        tile_event()
    for copy in bias_copies:
        copy.wait_recv()
    force = bias_in[0]
    for e in range(1, nc):
        force = force + bias_in[e]
    force_ref[...] = force
    field = (noise_ref[...] - SQRT_TAU * force).astype(bf16)
    lane2 = lax.broadcasted_iota(jnp.int32, (vec, 2 * slots), 1)
    mine = lane2 // slots == a % 2
    fits = (lane2 % slots < count_s[0]) & mine
    hot2 = jnp.where(
        fits & (lax.broadcasted_iota(jnp.int32, (vec, 2 * slots), 0) == vec2), 1.0, 0.0
    ).astype(bf16)
    tile_rows = row_ref[...]
    block = tile_rows // cols
    spot = ((block % 2) * ny + block // 2) * cols + tile_rows % cols
    place2 = jnp.concatenate([col_ref[...] * rblocks + spot] * 2, axis=1)
    spots = jnp.where(mine[:8], place2.astype(f32), 0.0)
    for g in range(ng):
        pick = lax.broadcasted_iota(jnp.int32, (pad, walk_all), 1) == (
            lax.broadcasted_iota(jnp.int32, (pad, walk_all), 0) * ng + g
        )
        fields = jnp.dot(pick.astype(f32).astype(bf16), field, preferred_element_type=f32)
        coeff = jnp.dot(fields.astype(bf16), hot2, preferred_element_type=f32)
        sent[g] = jnp.concatenate([coeff, spots], axis=0).astype(bf16)
    sent_copies = []
    for f in range(1, nw):
        copy = remote(
            sent.at[((a + f) % nw) % ng], got.at[a], g_s.at[f - 1], g_r.at[f - 1], w_peer(f)
        )
        copy.start()
        sent_copies.append(copy)
    got[a] = sent[x]
    for k in range(chunks * BEFORE // 8, chunks):
        tile_z(k)
    for _ in range(EVENTS[6]):
        tile_event()
    for copy in sent_copies:
        copy.wait_recv()

    def lanes(at):
        return jnp.concatenate(
            [got[2 * p].astype(f32)[at : at + 1] + got[2 * p + 1].astype(f32)[at : at + 1] for p in range(nw // 2)],
            axis=1,
        )

    hit = lax.broadcasted_iota(jnp.int32, (places, depth), 0) == lanes(pad).astype(jnp.int32)
    for w in range(group):
        wts[pl.ds(w * places, places), :] = jnp.where(hit, lanes(w), 0.0).astype(bf16)

    def op_at(h, w, col):
        return ((h * group + w) * cols + col) * rows

    def build(h):
        def one(j, carry):
            out = jnp.dot(wts[...], tin[j], preferred_element_type=f32)
            for w in range(group):
                for col in range(cols):
                    top = w * places + col * rblocks
                    at = op_at(h, w, col) + j - h * ROWS
                    op32[pl.ds(at, rblocks, stride=ROWS), :] = out[top : top + rblocks]
            return carry

        return one

    def build_chunk(k):
        for d in range(nr):
            for e in range(1, ng):
                tx[k, d, e].wait_recv()
        lax.fori_loop(k * part, (k + 1) * part, build(k * part // ROWS), 0)

    def narrow(h):
        for w in range(group):
            for col in range(cols):
                op[h, w, :, pl.ds(col * tb, tb)] = op32[pl.ds(op_at(h, w, col), rows), :].astype(bf16)

    items = [(0, w, h) for h in range(halves) for w in range(group)]
    items += [(k, w, h) for k in range(1, TAYLOR) for w in range(group) for h in range(halves)]
    spots_of = {item: t for t, item in enumerate(items)}
    waited = set()
    core_copy = {}
    y_copy = {}
    z_copy = {}

    def multiply(t):
        k, w, h = items[t]
        if k and (w, k) not in waited:
            waited.add((w, k))
            for g in range(halves):
                for d in range(1, nr):
                    z_wait(spots_of[k - 1, w, g], d)
        right = term[k, w].reshape(orb, nel)
        there = pl.ds(pl.multiple_of((1 - core) * half, half), half)
        here = pl.ds(pl.multiple_of(core * half, half), half)
        c_send[t] = jnp.dot(op[h, w, there, :], right, preferred_element_type=f32).astype(bf16)
        core_copy[t] = remote(
            c_send.at[t], c_recv.at[t], cs.at[t], cr.at[t], c_dev(y * 2 + 1 - core)
        )
        core_copy[t].start()
        own[t % 4] = jnp.dot(op[h, w, here, :], right, preferred_element_type=f32)

    def add_core(t):
        core_copy[t].wait_recv()
        for e in range(1, ny):
            to = (y + e) % ny
            at = pl.ds(pl.multiple_of(to * piece, piece), piece)
            y_send[t, e - 1] = (own[t % 4, at, :] + c_recv[t, at, :].astype(f32)).astype(bf16)
            y_copy[t, e] = remote(
                y_send.at[t, e - 1], y_recv.at[t, e - 1], ys.at[t, e - 1], yr.at[t, e - 1], c_dev(to * 2 + core)
            )
            y_copy[t, e].start()

    def relay(t):
        k, w, h = items[t]
        if k == TAYLOR - 1 or nr < 3:
            return
        for at_z, from_z, d in ((nr - 2, 0, nr - 2), (1, nr - 1, 2)):

            @pl.when(z == at_z)
            def _():
                z_send(t, d, from_z).wait_recv()
                relay_copy(t, from_z).start()

            later(z == at_z, lambda from_z=from_z: relay_copy(t, from_z).wait_send())

    def relay_copy(t, from_z):
        k, w, h = items[t]
        at = term.at[k + 1, w, :, from_z, h]
        d = nr - 1 if from_z == 0 else 1
        return remote(at, at, zs.at[k, w, h, nr - 1], zr.at[k, w, h, d - 1], z_dev(nr - 1 - from_z))

    def z_send(t, d, from_z):
        k, w, h = items[t]
        at = term.at[k + 1, w, :, from_z, h]
        return remote(at, at, zs.at[k, w, h, d - 1], zr.at[k, w, h, d - 1], z_dev((from_z + d) % nr))

    def far(d, sender):
        if nr < 3:
            return False
        if d == nr - 1:
            return sender == 0
        if d == 1:
            return sender == nr - 1
        return False

    def z_wait(t, d):
        here = (z + nr - d) % nr
        taken = False
        if nr >= 3:
            if d == nr - 2:
                taken = z == nr - 2
            if d == 2:
                taken = (z == 1) if taken is False else taken | (z == 1)
        if taken is False:
            z_send(t, d, here).wait_recv()
        else:

            @pl.when(jnp.logical_not(taken))
            def _():
                z_send(t, d, here).wait_recv()

    def finish(t):
        k, w, h = items[t]
        at = pl.ds(pl.multiple_of(y * piece, piece), piece)
        value = own[t % 4, at, :] + c_recv[t, at, :].astype(f32)
        for e in range(1, ny):
            y_copy[t, e].wait_recv()
            value = value + y_recv[t, e - 1].astype(f32)
        new = (SQRT_TAU / (k + 1) * value).astype(bf16)
        added = total[w, h] + new.astype(f32)
        if k < TAYLOR - 1:
            total[w, h] = added
            term[k + 1, w, :, z, h] = new.reshape(cols, ROWS, nel)
            for d in range(1, nr):
                skip = far(d, z)
                if skip is False:
                    z_send(t, d, z).start()
                    later(None, lambda d=d: z_send(t, d, z).wait_send())
                else:

                    @pl.when(jnp.logical_not(skip))
                    def _():
                        z_send(t, d, z).start()

                    later(jnp.logical_not(skip), lambda d=d: z_send(t, d, z).wait_send())
            return
        fin[w, h] = added.astype(bf16).reshape(cols, ROWS, nel)

        @pl.when(z == w)
        def _():
            out_ref[:, z, h] = fin[w, h]

        @pl.when(z != w)
        def _():
            remote(fin.at[w, h], out_ref.at[:, z, h], fs.at[w, h], fr.at[z, h], z_dev(w)).start()

    def run(first, last, tail):
        for t in range(first, last + LAG_RELAY):
            if first <= t - LAG_RELAY:
                relay(t - LAG_RELAY)
            if t < last:
                multiply(t)
            if first <= t - LAG_CORE < last:
                add_core(t - LAG_CORE)
            if first <= t - LAG_Y < last:
                finish(t - LAG_Y)
        return []

    tile_event()
    own_copy.wait()
    per = ROWS // part
    behind = []
    for h in range(halves):
        for k in range(h * per, (h + 1) * per):
            while todo and k >= todo[0]:
                tile_event()
            build_chunk(k)
            tile_event()
            if behind:
                relay(behind.pop(0))
        narrow(h)
        for t in behind:
            relay(t)
        behind = []
        if h < halves - 1:
            behind = run(h * group, (h + 1) * group, False)
    run((halves - 1) * group, len(items), True)
    for w in range(group):

        @pl.when(z != w)
        def _():
            for h in range(halves):
                copy = remote(fin.at[w, h], out_ref.at[:, w, h], fs.at[w, h], fr.at[w, h], z_dev(w))
                copy.wait_send()
                copy.wait_recv()

    for s in range(nr - 1):
        passed(s, 0)
        passed(s, 1)
    for zz in range(nr):
        for e in range(1, ng):
            for h in range(PARTS):
                walk_x(zz, e, h).wait_send()
    for s in range(nw):
        for f in range(1, nc):
            inverse_copy(s, f).wait_send()
    for copy in list(tz.values()) + list(tx.values()) + bias_copies + sent_copies:
        copy.wait_send()
    for copy in list(core_copy.values()) + list(y_copy.values()):
        copy.wait_send()
    for condition, action in ends:
        if condition is None:
            action()
        else:
            pl.when(condition)(action)


def step(row, col, vector, count, sources, walkers, inv, trial, tiles, noise, nr, ng, nc):
    f32 = jnp.float32
    bf16 = jnp.bfloat16
    nw = nr * ng
    orb, nel = walkers.shape
    slots, tb, _ = tiles.shape
    walk_all, vec = noise.shape
    group = walk_all // ng
    cols = orb // tb
    q = nel // nc
    pad = (group + 7) // 8 * 8
    j = tb // nr
    chunks = j // CHUNK
    rblocks = trial.shape[0]
    halves = j // ROWS
    rows = rblocks * ROWS
    piece = rows // nc
    more = max(nc // 2 - 1, 1)
    items = TAYLOR * group * halves
    dma = pltpu.SemaphoreType.DMA
    vmem = pl.BlockSpec(memory_space=pltpu.VMEM)
    smem = pl.BlockSpec(memory_space=pltpu.SMEM)
    hbm = pl.BlockSpec(memory_space=pl.ANY)

    def both(*shape):
        return [dma(shape), dma(shape)]

    return pl.pallas_call(
        functools.partial(step_kernel, nr, ng, nc),
        out_shape=(
            jax.ShapeDtypeStruct((walk_all, vec), f32),
            jax.ShapeDtypeStruct((cols, nr, halves, ROWS, nel), bf16),
        ),
        in_specs=[smem] * 4 + [hbm] * 4 + [vmem] * 4,
        out_specs=(vmem, vmem),
        scratch_shapes=[
            pltpu.VMEM((nw, orb + q, nel), bf16),
            pltpu.VMEM((nw, nel, nel), bf16),
            pltpu.VMEM((slots, tb, nel), bf16),
            pltpu.VMEM((walk_all, cols, tb, nel), f32),
            pltpu.VMEM((walk_all, slots, 128), f32),
            pltpu.VMEM((nc, walk_all, vec), f32),
            pltpu.VMEM((ng, pad + 8, 2 * slots), bf16),
            pltpu.VMEM((nw, pad + 8, 2 * slots), bf16),
            pltpu.VMEM((j, nw * slots, tb), bf16),
            pltpu.VMEM((group * cols * rblocks, nw * slots), bf16),
            pltpu.VMEM((max(halves * group * cols * rows, slots * tb), tb), f32),
            pltpu.VMEM((halves, group, rows, orb), bf16),
            pltpu.VMEM((TAYLOR, group, cols, nr, halves, ROWS, nel), bf16),
            pltpu.VMEM((group, halves, piece, nel), f32),
            pltpu.VMEM((4, rows // 2, nel), f32),
            pltpu.VMEM((items, rows // 2, nel), bf16),
            pltpu.VMEM((items, rows // 2, nel), bf16),
            pltpu.VMEM((items, more, piece, nel), bf16),
            pltpu.VMEM((items, more, piece, nel), bf16),
            pltpu.VMEM((group, halves, cols, ROWS, nel), bf16),
            pltpu.VMEM(trial.shape, bf16),
            pltpu.VMEM(tiles.shape, bf16),
            pltpu.VMEM((tb, slots, tb), bf16),
            dma((4,)),
        ]
        + both(nr - 1, PARTS)
        + both(nr - 1, PARTS)
        + both(ng - 1, nr, PARTS)
        + both(nw, nc - 1)
        + both(chunks, nr - 1)
        + both(ng - 1, chunks, nr)
        + [dma]
        + both(nc - 1)
        + both(nw - 1)
        + both(items)
        + both(items, more)
        + both(TAYLOR - 1, group, halves, nr)
        + both(group, halves),
        compiler_params=pltpu.CompilerParams(
            collective_id=0, has_side_effects=True, vmem_limit_bytes=VMEM_LIMIT
        ),
    )(
        row,
        col,
        count,
        sources,
        walkers,
        inv,
        trial,
        tiles,
        noise,
        vector.reshape(1, slots),
        row.reshape(1, slots),
        col.reshape(1, slots),
    )


def body(
    walkers,
    intersection_inv,
    trial_state,
    chol_tiles,
    tile_vector,
    tile_row,
    tile_col,
    tile_count,
    sources,
    aux_noise,
):
    _, orb, nel = walkers.shape
    tb = chol_tiles.shape[1]
    rblocks = trial_state.shape[0] // tb
    wide = lax.axis_size("wide")
    nc = lax.axis_size("chol")
    nr, ng = split_wide(wide, tb)
    force, out = step(
        tile_row,
        tile_col,
        tile_vector,
        tile_count,
        sources,
        walkers[0],
        intersection_inv[0],
        trial_state.reshape(rblocks, tb, nel),
        chol_tiles,
        aux_noise,
        nr,
        ng,
        nc,
    )
    return (force, out.reshape(1, orb, nel))


def solution(mesh):
    return jax.shard_map(
        body,
        mesh=mesh,
        in_specs=(
            P("wide", "chol", None),
            P("wide", None, None),
            P(),
            P(("wide", "chol"), None, None),
            P(("wide", "chol")),
            P(("wide", "chol")),
            P(("wide", "chol")),
            P(("wide", "chol")),
            P(),
            P(None, "wide"),
        ),
        out_specs=(P(None, "wide"), P("wide", "chol", None)),
        check_vma=False,
    )
```

```python
import functools

import jax
import jax.numpy as jnp
from jax import lax
from jax.experimental import pallas as pl
from jax.experimental.pallas import tpu as pltpu
from jax.sharding import PartitionSpec as P

TAYLOR = 4


SQRT_TAU = 0.1
MESH = pl.DeviceIdType.MESH
VMEM_LIMIT = 60 * 1024 * 1024
CHUNK = 4
OWN_FIRST = 2
EVENTS = (1, 0, 1, 0, 1, 0, 1)
BEFORE = 6
ROWS = 16
PARTS = 3
LAG_CORE = 1
LAG_Y = 2
LAG_RELAY = 3


def split_wide(wide, tile_size):
    parts = min(wide // 2, tile_size // 16)
    return parts, wide // parts


def remote(src, dst, send, recv, device):
    return pltpu.make_async_remote_copy(
        src_ref=src, dst_ref=dst, send_sem=send, recv_sem=recv, device_id=device, device_id_type=MESH
    )


def meet(peers):
    barrier = pltpu.get_barrier_semaphore()
    for peer in peers:
        pl.semaphore_signal(barrier, inc=1, device_id=peer, device_id_type=MESH)
    return lambda: pl.semaphore_wait(barrier, len(peers))


def step_kernel(
    nr,
    ng,
    nc,
    row_s,
    col_s,
    count_s,
    src_s,
    walk_ref,
    inv_ref,
    trial_hbm,
    tiles_hbm,
    noise_ref,
    vec_ref,
    row_ref,
    col_ref,
    force_ref,
    out_ref,
    blk,
    inv_all,
    proj,
    theta,
    scores,
    bias_in,
    sent,
    got,
    tin,
    wts,
    op32,
    op,
    term,
    total,
    own,
    c_send,
    c_recv,
    y_send,
    y_recv,
    fin,
    trial_ref,
    tiles_ref,
    cut,
    load_s,
    wu_s,
    wu_r,
    wd_s,
    wd_r,
    wx_s,
    wx_r,
    iq_s,
    iq_r,
    tz_s,
    tz_r,
    tx_s,
    tx_r,
    own_s,
    b_s,
    b_r,
    g_s,
    g_r,
    cs,
    cr,
    ys,
    yr,
    zs,
    zr,
    fs,
    fr,
):
    f32 = jnp.float32
    bf16 = jnp.bfloat16
    nw = nr * ng
    ny = nc // 2
    a = lax.axis_index("wide")
    c = lax.axis_index("chol")
    z = a // ng
    x = a % ng
    core = c % 2
    y = c // 2
    orb, nel = walk_ref.shape
    q = nel // nc
    slots, tb, _ = tiles_ref.shape
    walk_all, vec = noise_ref.shape
    group = walk_all // ng
    cols = orb // tb
    j_all = tb // nr
    part = CHUNK
    chunks = j_all // part
    depth = nw * slots
    halves = j_all // ROWS
    rblocks = trial_ref.shape[0]
    rows = rblocks * ROWS
    piece = rows // nc
    half = rows // 2
    places = cols * rblocks
    pad = sent.shape[1] - 8

    def z_dev(to):
        return (to * ng + x, c)

    def x_dev(e):
        return (z * ng + (x + e) % ng, c)

    def c_dev(to):
        return (a, to)

    def c_peer(e):
        return (a, (c + e) % nc)

    def w_peer(f):
        return ((a + f) % nw, c)

    def slab(d, e):
        return ((z + nr - d) % nr) * ng + (x + ng - e) % ng

    ends = []

    def later(condition, action):
        ends.append((condition, action))

    q_at = pl.ds(pl.multiple_of(c * q, 16), q)
    loads = [
        pltpu.make_async_copy(src, dst, load_s.at[n])
        for n, (src, dst) in enumerate(
            (
                (walk_ref, blk.at[a, pl.ds(0, orb)]),
                (inv_ref.at[q_at], blk.at[a, pl.ds(orb, q)]),
                (tiles_hbm, tiles_ref),
                (trial_hbm, trial_ref),
            )
        )
    ]
    for load in loads:
        load.start()
    wait_all = meet([w_peer(f) for f in range(1, nw)] + [c_peer(e) for e in range(1, nc)])
    loads[0].wait()
    loads[1].wait()
    wait_all()

    def has(s, side):
        return z - s >= 0 if side == 0 else z + s < nr

    def source(s, side):
        return z - s if side == 0 else z + s

    span = (orb + q) // PARTS

    def link(s, side, h):
        at = blk.at[source(s, side) * ng + x, pl.ds(h * span, span)]
        send, recv = (wu_s, wu_r) if side == 0 else (wd_s, wd_r)
        return lambda i: remote(
            at, at, send.at[i, h], recv.at[i, h], z_dev((z + 1) % nr if side == 0 else (z + nr - 1) % nr)
        )

    def pass_on(s, side, h):
        ahead = z + 1 < nr if side == 0 else z - 1 >= 0

        @pl.when(has(s, side) & ahead)
        def _():
            link(s, side, h)(s).start()

    def passed(s, side):
        ahead = z + 1 < nr if side == 0 else z - 1 >= 0

        @pl.when(has(s, side) & ahead)
        def _():
            for h in range(PARTS):
                link(s, side, h)(s).wait_send()

    def walk_x(zz, e, h):
        at = blk.at[zz * ng + x, pl.ds(h * span, span)]
        return remote(at, at, wx_s.at[e - 1, zz, h], wx_r.at[e - 1, zz, h], x_dev(e))

    def inverse_copy(s, f):
        return remote(
            blk.at[s, pl.ds(orb, q)],
            inv_all.at[s, q_at],
            iq_s.at[s, f - 1],
            iq_r.at[s, f - 1],
            c_peer(f),
        )

    def inverse(s):
        inv_all[s, q_at, :] = blk[s, pl.ds(orb, q), :]
        for f in range(1, nc):
            inverse_copy(s, f).start()

    def arrive(s, side, h):
        @pl.when(has(s, side))
        def _():
            link(s, side, h)(s - 1).wait_recv()

        if s < nr - 1:
            pass_on(s, side, h)

        @pl.when(has(s, side))
        def _():
            zz = source(s, side)
            for e in range(1, ng):
                walk_x(zz, e, h).start()
            if h == PARTS - 1:
                inverse(zz * ng + x)

    def tile_at(k, s):
        return tin.at[pl.ds(k * part, part), pl.ds(pl.multiple_of(s * slots, slots), slots), :]

    def cut_at(k, to):
        return cut.at[pl.ds(to * j_all + k * part, part)]

    tz = {}
    tx = {}

    def tile_z(k):
        for d in sorted(range(1, nr), key=lambda d: abs(d - nr / 2)):
            tz[k, d] = remote(
                cut_at(k, (z + d) % nr), tile_at(k, a), tz_s.at[k, d - 1], tz_r.at[k, d - 1], z_dev((z + d) % nr)
            )
            tz[k, d].start()

    def tile_x(k, d):
        at = tile_at(k, slab(d, 0))
        for e in range(1, ng):
            tx[k, d, e] = remote(
                cut_at(k, z) if d == 0 else at, at, tx_s.at[e - 1, k, d], tx_r.at[e - 1, k, d], x_dev(e)
            )
            tx[k, d, e].start()

    todo = list(range(chunks))

    def tile_event():
        if not todo or (todo[0], 1) not in tz:
            return
        k = todo.pop(0)
        for d in sorted(range(1, nr), key=lambda d: -abs(d - nr / 2)):
            tz[k, d].wait_recv()
            tile_x(k, d)

    for h in reversed(range(PARTS)):
        pass_on(0, 0, h)
        pass_on(0, 1, h)
        for e in range(1, ng):
            walk_x(z, e, h).start()
    inverse(a)
    loads[2].wait()

    def spread(i, carry):
        op32[pl.ds(i, tb, stride=slots), :] = tiles_ref[i].astype(f32)
        return carry

    def collect(p, carry):
        cut[p] = op32[pl.ds(pl.multiple_of(p * slots, slots), slots), :].astype(bf16)
        return carry

    lax.fori_loop(0, slots, spread, 0, unroll=2)
    lax.fori_loop(0, tb, collect, 0, unroll=4)
    for k in range(chunks * OWN_FIRST // 8):
        tile_x(k, 0)
    own_copy = pltpu.make_async_copy(
        cut.at[pl.ds(z * j_all, j_all)], tin.at[:, pl.ds(pl.multiple_of(a * slots, slots), slots), :], own_s
    )
    own_copy.start()
    loads[3].wait()

    def project(i, carry):
        out = lax.dot_general(
            tiles_ref[i], trial_ref[row_s[i]], (((0,), (0,)), ((), ())), preferred_element_type=f32
        )
        proj[i] = out.astype(bf16)
        return carry

    cuts = [slots * d // nr for d in range(nr + 1)]
    for s in range(1, nr):
        lax.fori_loop(cuts[s - 1], cuts[s], project, 0)
        for h in reversed(range(PARTS)):
            arrive(s, 0, h)
            arrive(s, 1, h)
        if s == min(2, nr - 1):
            for k in range(chunks * 2 // 8):
                tile_z(k)
    lax.fori_loop(cuts[nr - 1], cuts[nr], project, 0)
    for k in range(chunks * OWN_FIRST // 8, chunks):
        tile_x(k, 0)
    for k in range(chunks * 2 // 8, chunks * BEFORE // 8):
        tile_z(k)
    for _ in range(EVENTS[0]):
        tile_event()
    for e in range(1, ng):
        for zz in range(nr):
            if zz == nr // 2:
                for _ in range(EVENTS[1]):
                    tile_event()
            for h in range(PARTS):
                walk_x(zz, e, h).wait_recv()
            inverse(zz * ng + (x + ng - e) % ng)
    for _ in range(EVENTS[2]):
        tile_event()
    for s in range(nw):
        for f in range(1, nc):
            inverse_copy(s, f).wait_recv()

    def make_theta(j, carry):
        src = src_s[j]
        out = jnp.dot(blk[src, pl.ds(0, orb), :], inv_all[src], preferred_element_type=f32)
        theta[j] = out.astype(bf16).astype(f32).reshape(cols, tb, nel)
        return carry

    lax.fori_loop(0, walk_all, make_theta, 0)
    for _ in range(EVENTS[3]):
        tile_event()

    def score_tile(i, carry):
        tile = proj[i].astype(f32)
        column = col_s[i]

        def one(w, inner):
            value = (tile * theta[w, column]).reshape(tb // 8, 8, nel)
            value = jnp.sum(value, axis=0)
            lanes = value[:, :128]
            for n in range(128, nel, 128):
                lanes = lanes + value[:, n : n + 128]
            scores[w, pl.ds(i, 1), :] = jnp.sum(lanes, axis=0, keepdims=True)
            return inner

        lax.fori_loop(0, walk_all, one, 0, unroll=8)
        return carry

    lax.fori_loop(0, slots // 2, score_tile, 0)
    for _ in range(EVENTS[4]):
        tile_event()
    lax.fori_loop(slots // 2, slots, score_tile, 0)

    ones = jnp.ones((walk_all, 128), bf16)
    across = (((1,), (1,)), ((), ()))

    def dot2(value, other, flip):
        high = value.astype(bf16)
        low = (value - high.astype(f32)).astype(bf16)
        return sum(
            lax.dot_general(*((other, v) if flip else (v, other)), across, preferred_element_type=f32)
            for v in (high, low)
        )

    each = dot2(scores[...].reshape(walk_all * slots, 128), ones, True)
    lane = lax.broadcasted_iota(jnp.int32, each.shape, 1)
    keep = (lane // slots == lax.broadcasted_iota(jnp.int32, each.shape, 0)) & (
        lane % slots < count_s[0]
    )
    vec2 = jnp.concatenate([vec_ref[...]] * 2, axis=1)
    hot = (lax.broadcasted_iota(jnp.int32, (vec, 2 * slots), 0) == vec2).astype(f32).astype(bf16)
    hot = jnp.concatenate([hot] * (walk_all // 2), axis=1)
    bias_in[c] = dot2(jnp.where(keep, each, 0.0), hot, False)
    bias_copies = []
    for e in range(1, nc):
        at = bias_in.at[c]
        copy = remote(at, at, b_s.at[e - 1], b_r.at[e - 1], c_peer(e))
        copy.start()
        bias_copies.append(copy)
    for k in range(group):
        first = blk[src_s[k * ng + x], pl.ds(0, orb), :]
        term[0, k] = first.reshape(cols, nr, halves, ROWS, nel)
        for h in range(halves):
            total[k, h] = term[0, k, :, z, h].astype(f32).reshape(piece, nel)
    for _ in range(EVENTS[5]):
        tile_event()
    for copy in bias_copies:
        copy.wait_recv()
    force = bias_in[0]
    for e in range(1, nc):
        force = force + bias_in[e]
    force_ref[...] = force
    field = (noise_ref[...] - SQRT_TAU * force).astype(bf16)
    lane2 = lax.broadcasted_iota(jnp.int32, (vec, 2 * slots), 1)
    mine = lane2 // slots == a % 2
    fits = (lane2 % slots < count_s[0]) & mine
    hot2 = jnp.where(
        fits & (lax.broadcasted_iota(jnp.int32, (vec, 2 * slots), 0) == vec2), 1.0, 0.0
    ).astype(bf16)
    tile_rows = row_ref[...]
    block = tile_rows // cols
    spot = ((block % 2) * ny + block // 2) * cols + tile_rows % cols
    place2 = jnp.concatenate([col_ref[...] * rblocks + spot] * 2, axis=1)
    spots = jnp.where(mine[:8], place2.astype(f32), 0.0)
    for g in range(ng):
        pick = lax.broadcasted_iota(jnp.int32, (pad, walk_all), 1) == (
            lax.broadcasted_iota(jnp.int32, (pad, walk_all), 0) * ng + g
        )
        fields = jnp.dot(pick.astype(f32).astype(bf16), field, preferred_element_type=f32)
        coeff = jnp.dot(fields.astype(bf16), hot2, preferred_element_type=f32)
        sent[g] = jnp.concatenate([coeff, spots], axis=0).astype(bf16)
    sent_copies = []
    for f in range(1, nw):
        copy = remote(
            sent.at[((a + f) % nw) % ng], got.at[a], g_s.at[f - 1], g_r.at[f - 1], w_peer(f)
        )
        copy.start()
        sent_copies.append(copy)
    got[a] = sent[x]
    for k in range(chunks * BEFORE // 8, chunks):
        tile_z(k)
    for _ in range(EVENTS[6]):
        tile_event()
    for copy in sent_copies:
        copy.wait_recv()

    def lanes(at):
        return jnp.concatenate(
            [got[2 * p].astype(f32)[at : at + 1] + got[2 * p + 1].astype(f32)[at : at + 1] for p in range(nw // 2)],
            axis=1,
        )

    hit = lax.broadcasted_iota(jnp.int32, (places, depth), 0) == lanes(pad).astype(jnp.int32)
    for w in range(group):
        wts[pl.ds(w * places, places), :] = jnp.where(hit, lanes(w), 0.0).astype(bf16)

    def op_at(h, w, col):
        return ((h * group + w) * cols + col) * rows

    def build(h):
        def one(j, carry):
            out = jnp.dot(wts[...], tin[j], preferred_element_type=f32)
            for w in range(group):
                for col in range(cols):
                    top = w * places + col * rblocks
                    at = op_at(h, w, col) + j - h * ROWS
                    op32[pl.ds(at, rblocks, stride=ROWS), :] = out[top : top + rblocks]
            return carry

        return one

    def build_chunk(k):
        for d in range(nr):
            for e in range(1, ng):
                tx[k, d, e].wait_recv()
        lax.fori_loop(k * part, (k + 1) * part, build(k * part // ROWS), 0)

    def narrow(h):
        for w in range(group):
            for col in range(cols):
                op[h, w, :, pl.ds(col * tb, tb)] = op32[pl.ds(op_at(h, w, col), rows), :].astype(bf16)

    items = [(0, w, h) for h in range(halves) for w in range(group)]
    items += [(k, w, h) for k in range(1, TAYLOR) for w in range(group) for h in range(halves)]
    spots_of = {item: t for t, item in enumerate(items)}
    waited = set()
    core_copy = {}
    y_copy = {}
    z_copy = {}

    def multiply(t):
        k, w, h = items[t]
        if k and (w, k) not in waited:
            waited.add((w, k))
            for g in range(halves):
                for d in range(1, nr):
                    z_wait(spots_of[k - 1, w, g], d)
        right = term[k, w].reshape(orb, nel)
        there = pl.ds(pl.multiple_of((1 - core) * half, half), half)
        here = pl.ds(pl.multiple_of(core * half, half), half)
        c_send[t] = jnp.dot(op[h, w, there, :], right, preferred_element_type=f32).astype(bf16)
        core_copy[t] = remote(
            c_send.at[t], c_recv.at[t], cs.at[t], cr.at[t], c_dev(y * 2 + 1 - core)
        )
        core_copy[t].start()
        own[t % 4] = jnp.dot(op[h, w, here, :], right, preferred_element_type=f32)

    def add_core(t):
        core_copy[t].wait_recv()
        for e in range(1, ny):
            to = (y + e) % ny
            at = pl.ds(pl.multiple_of(to * piece, piece), piece)
            y_send[t, e - 1] = (own[t % 4, at, :] + c_recv[t, at, :].astype(f32)).astype(bf16)
            y_copy[t, e] = remote(
                y_send.at[t, e - 1], y_recv.at[t, e - 1], ys.at[t, e - 1], yr.at[t, e - 1], c_dev(to * 2 + core)
            )
            y_copy[t, e].start()

    def relay(t):
        k, w, h = items[t]
        if k == TAYLOR - 1 or nr < 3:
            return
        for at_z, from_z, d in ((nr - 2, 0, nr - 2), (1, nr - 1, 2)):

            @pl.when(z == at_z)
            def _():
                z_send(t, d, from_z).wait_recv()
                relay_copy(t, from_z).start()

            later(z == at_z, lambda from_z=from_z: relay_copy(t, from_z).wait_send())

    def relay_copy(t, from_z):
        k, w, h = items[t]
        at = term.at[k + 1, w, :, from_z, h]
        d = nr - 1 if from_z == 0 else 1
        return remote(at, at, zs.at[k, w, h, nr - 1], zr.at[k, w, h, d - 1], z_dev(nr - 1 - from_z))

    def z_send(t, d, from_z):
        k, w, h = items[t]
        at = term.at[k + 1, w, :, from_z, h]
        return remote(at, at, zs.at[k, w, h, d - 1], zr.at[k, w, h, d - 1], z_dev((from_z + d) % nr))

    def far(d, sender):
        if nr < 3:
            return False
        if d == nr - 1:
            return sender == 0
        if d == 1:
            return sender == nr - 1
        return False

    def z_wait(t, d):
        here = (z + nr - d) % nr
        taken = False
        if nr >= 3:
            if d == nr - 2:
                taken = z == nr - 2
            if d == 2:
                taken = (z == 1) if taken is False else taken | (z == 1)
        if taken is False:
            z_send(t, d, here).wait_recv()
        else:

            @pl.when(jnp.logical_not(taken))
            def _():
                z_send(t, d, here).wait_recv()

    def finish(t):
        k, w, h = items[t]
        at = pl.ds(pl.multiple_of(y * piece, piece), piece)
        value = own[t % 4, at, :] + c_recv[t, at, :].astype(f32)
        for e in range(1, ny):
            y_copy[t, e].wait_recv()
            value = value + y_recv[t, e - 1].astype(f32)
        new = (SQRT_TAU / (k + 1) * value).astype(bf16)
        added = total[w, h] + new.astype(f32)
        if k < TAYLOR - 1:
            total[w, h] = added
            term[k + 1, w, :, z, h] = new.reshape(cols, ROWS, nel)
            for d in sorted(range(1, nr), key=lambda d: abs(d - nr / 2)):
                skip = far(d, z)
                if skip is False:
                    z_send(t, d, z).start()
                    later(None, lambda d=d: z_send(t, d, z).wait_send())
                else:

                    @pl.when(jnp.logical_not(skip))
                    def _():
                        z_send(t, d, z).start()

                    later(jnp.logical_not(skip), lambda d=d: z_send(t, d, z).wait_send())
            return
        fin[w, h] = added.astype(bf16).reshape(cols, ROWS, nel)

        @pl.when(z == w)
        def _():
            out_ref[:, z, h] = fin[w, h]

        @pl.when(z != w)
        def _():
            remote(fin.at[w, h], out_ref.at[:, z, h], fs.at[w, h], fr.at[z, h], z_dev(w)).start()

    def run(first, last, tail):
        for t in range(first, last + LAG_RELAY):
            if first <= t - LAG_RELAY:
                relay(t - LAG_RELAY)
            if t < last:
                multiply(t)
            if first <= t - LAG_CORE < last:
                add_core(t - LAG_CORE)
            if first <= t - LAG_Y < last:
                finish(t - LAG_Y)
        return []

    tile_event()
    own_copy.wait()
    per = ROWS // part
    behind = []
    for h in range(halves):
        for k in range(h * per, (h + 1) * per):
            while todo and k >= todo[0]:
                tile_event()
            build_chunk(k)
            tile_event()
            if behind:
                relay(behind.pop(0))
        narrow(h)
        for t in behind:
            relay(t)
        behind = []
        if h < halves - 1:
            behind = run(h * group, (h + 1) * group, False)
    run((halves - 1) * group, len(items), True)
    for w in range(group):

        @pl.when(z != w)
        def _():
            for h in range(halves):
                copy = remote(fin.at[w, h], out_ref.at[:, w, h], fs.at[w, h], fr.at[w, h], z_dev(w))
                copy.wait_send()
                copy.wait_recv()

    for s in range(nr - 1):
        passed(s, 0)
        passed(s, 1)
    for zz in range(nr):
        for e in range(1, ng):
            for h in range(PARTS):
                walk_x(zz, e, h).wait_send()
    for s in range(nw):
        for f in range(1, nc):
            inverse_copy(s, f).wait_send()
    for copy in list(tz.values()) + list(tx.values()) + bias_copies + sent_copies:
        copy.wait_send()
    for copy in list(core_copy.values()) + list(y_copy.values()):
        copy.wait_send()
    for condition, action in ends:
        if condition is None:
            action()
        else:
            pl.when(condition)(action)


def step(row, col, vector, count, sources, walkers, inv, trial, tiles, noise, nr, ng, nc):
    f32 = jnp.float32
    bf16 = jnp.bfloat16
    nw = nr * ng
    orb, nel = walkers.shape
    slots, tb, _ = tiles.shape
    walk_all, vec = noise.shape
    group = walk_all // ng
    cols = orb // tb
    q = nel // nc
    pad = (group + 7) // 8 * 8
    j = tb // nr
    chunks = j // CHUNK
    rblocks = trial.shape[0]
    halves = j // ROWS
    rows = rblocks * ROWS
    piece = rows // nc
    more = max(nc // 2 - 1, 1)
    items = TAYLOR * group * halves
    dma = pltpu.SemaphoreType.DMA
    vmem = pl.BlockSpec(memory_space=pltpu.VMEM)
    smem = pl.BlockSpec(memory_space=pltpu.SMEM)
    hbm = pl.BlockSpec(memory_space=pl.ANY)

    def both(*shape):
        return [dma(shape), dma(shape)]

    return pl.pallas_call(
        functools.partial(step_kernel, nr, ng, nc),
        out_shape=(
            jax.ShapeDtypeStruct((walk_all, vec), f32),
            jax.ShapeDtypeStruct((cols, nr, halves, ROWS, nel), bf16),
        ),
        in_specs=[smem] * 4 + [hbm] * 4 + [vmem] * 4,
        out_specs=(vmem, vmem),
        scratch_shapes=[
            pltpu.VMEM((nw, orb + q, nel), bf16),
            pltpu.VMEM((nw, nel, nel), bf16),
            pltpu.VMEM((slots, tb, nel), bf16),
            pltpu.VMEM((walk_all, cols, tb, nel), f32),
            pltpu.VMEM((walk_all, slots, 128), f32),
            pltpu.VMEM((nc, walk_all, vec), f32),
            pltpu.VMEM((ng, pad + 8, 2 * slots), bf16),
            pltpu.VMEM((nw, pad + 8, 2 * slots), bf16),
            pltpu.VMEM((j, nw * slots, tb), bf16),
            pltpu.VMEM((group * cols * rblocks, nw * slots), bf16),
            pltpu.VMEM((max(halves * group * cols * rows, slots * tb), tb), f32),
            pltpu.VMEM((halves, group, rows, orb), bf16),
            pltpu.VMEM((TAYLOR, group, cols, nr, halves, ROWS, nel), bf16),
            pltpu.VMEM((group, halves, piece, nel), f32),
            pltpu.VMEM((4, rows // 2, nel), f32),
            pltpu.VMEM((items, rows // 2, nel), bf16),
            pltpu.VMEM((items, rows // 2, nel), bf16),
            pltpu.VMEM((items, more, piece, nel), bf16),
            pltpu.VMEM((items, more, piece, nel), bf16),
            pltpu.VMEM((group, halves, cols, ROWS, nel), bf16),
            pltpu.VMEM(trial.shape, bf16),
            pltpu.VMEM(tiles.shape, bf16),
            pltpu.VMEM((tb, slots, tb), bf16),
            dma((4,)),
        ]
        + both(nr - 1, PARTS)
        + both(nr - 1, PARTS)
        + both(ng - 1, nr, PARTS)
        + both(nw, nc - 1)
        + both(chunks, nr - 1)
        + both(ng - 1, chunks, nr)
        + [dma]
        + both(nc - 1)
        + both(nw - 1)
        + both(items)
        + both(items, more)
        + both(TAYLOR - 1, group, halves, nr)
        + both(group, halves),
        compiler_params=pltpu.CompilerParams(
            collective_id=0, has_side_effects=True, vmem_limit_bytes=VMEM_LIMIT
        ),
    )(
        row,
        col,
        count,
        sources,
        walkers,
        inv,
        trial,
        tiles,
        noise,
        vector.reshape(1, slots),
        row.reshape(1, slots),
        col.reshape(1, slots),
    )


def settle_kernel(force_in, out_in, force_out, out_out):
    force_out[...] = force_in[...]
    out_out[...] = out_in[...]


def settle(force, out):
    vmem = pl.BlockSpec(memory_space=pltpu.VMEM)
    return pl.pallas_call(
        settle_kernel,
        out_shape=tuple(jax.ShapeDtypeStruct(v.shape, v.dtype) for v in (force, out)),
        in_specs=[vmem] * 2,
        out_specs=(vmem,) * 2,
    )(force, out)


def body(
    walkers,
    intersection_inv,
    trial_state,
    chol_tiles,
    tile_vector,
    tile_row,
    tile_col,
    tile_count,
    sources,
    aux_noise,
):
    _, orb, nel = walkers.shape
    tb = chol_tiles.shape[1]
    rblocks = trial_state.shape[0] // tb
    wide = lax.axis_size("wide")
    nc = lax.axis_size("chol")
    nr, ng = split_wide(wide, tb)
    force, out = step(
        tile_row,
        tile_col,
        tile_vector,
        tile_count,
        sources,
        walkers[0],
        intersection_inv[0],
        trial_state.reshape(rblocks, tb, nel),
        chol_tiles,
        aux_noise,
        nr,
        ng,
        nc,
    )
    return settle(force, out.reshape(1, orb, nel))


def solution(mesh):
    return jax.shard_map(
        body,
        mesh=mesh,
        in_specs=(
            P("wide", "chol", None),
            P("wide", None, None),
            P(),
            P(("wide", "chol"), None, None),
            P(("wide", "chol")),
            P(("wide", "chol")),
            P(("wide", "chol")),
            P(("wide", "chol")),
            P(),
            P(None, "wide"),
        ),
        out_specs=(P(None, "wide"), P("wide", "chol", None)),
        check_vma=False,
    )
```

```python
import functools

import jax
import jax.numpy as jnp
from jax import lax
from jax.experimental import pallas as pl
from jax.experimental.pallas import tpu as pltpu
from jax.sharding import PartitionSpec as P

TAYLOR = 4


SQRT_TAU = 0.1
MESH = pl.DeviceIdType.MESH
VMEM_LIMIT = 60 * 1024 * 1024
CHUNK = 4
OWN_FIRST = 2
EVENTS = (1, 1, 0, 0, 1, 0, 1)
BEFORE = 6
ROWS = 16
PARTS = 3
LAG_CORE = 1
LAG_Y = 2
LAG_RELAY = 3


def split_wide(wide, tile_size):
    parts = min(wide // 2, tile_size // 16)
    return parts, wide // parts


def remote(src, dst, send, recv, device):
    return pltpu.make_async_remote_copy(
        src_ref=src, dst_ref=dst, send_sem=send, recv_sem=recv, device_id=device, device_id_type=MESH
    )


def meet(peers):
    barrier = pltpu.get_barrier_semaphore()
    for peer in peers:
        pl.semaphore_signal(barrier, inc=1, device_id=peer, device_id_type=MESH)
    return lambda: pl.semaphore_wait(barrier, len(peers))


def step_kernel(
    nr,
    ng,
    nc,
    row_s,
    col_s,
    count_s,
    src_s,
    walk_ref,
    inv_ref,
    trial_hbm,
    tiles_hbm,
    noise_ref,
    vec_ref,
    row_ref,
    col_ref,
    force_ref,
    out_ref,
    blk,
    inv_all,
    proj,
    theta,
    scores,
    bias_in,
    sent,
    got,
    tin,
    wts,
    op32,
    op,
    term,
    total,
    own,
    c_send,
    c_recv,
    y_send,
    y_recv,
    fin,
    trial_ref,
    tiles_ref,
    cut,
    load_s,
    wu_s,
    wu_r,
    wd_s,
    wd_r,
    wx_s,
    wx_r,
    iq_s,
    iq_r,
    tz_s,
    tz_r,
    tx_s,
    tx_r,
    own_s,
    b_s,
    b_r,
    g_s,
    g_r,
    cs,
    cr,
    ys,
    yr,
    zs,
    zr,
    fs,
    fr,
):
    f32 = jnp.float32
    bf16 = jnp.bfloat16
    nw = nr * ng
    ny = nc // 2
    a = lax.axis_index("wide")
    c = lax.axis_index("chol")
    z = a // ng
    x = a % ng
    core = c % 2
    y = c // 2
    orb, nel = walk_ref.shape
    q = nel // nc
    slots, tb, _ = tiles_ref.shape
    walk_all, vec = noise_ref.shape
    group = walk_all // ng
    cols = orb // tb
    j_all = tb // nr
    part = CHUNK
    chunks = j_all // part
    depth = nw * slots
    halves = j_all // ROWS
    rblocks = trial_ref.shape[0]
    rows = rblocks * ROWS
    piece = rows // nc
    half = rows // 2
    places = cols * rblocks
    pad = sent.shape[1] - 8

    def z_dev(to):
        return (to * ng + x, c)

    def x_dev(e):
        return (z * ng + (x + e) % ng, c)

    def c_dev(to):
        return (a, to)

    def c_peer(e):
        return (a, (c + e) % nc)

    def w_peer(f):
        return ((a + f) % nw, c)

    def slab(d, e):
        return ((z + nr - d) % nr) * ng + (x + ng - e) % ng

    ends = []

    def later(condition, action):
        ends.append((condition, action))

    q_at = pl.ds(pl.multiple_of(c * q, 16), q)
    loads = [
        pltpu.make_async_copy(src, dst, load_s.at[n])
        for n, (src, dst) in enumerate(
            (
                (walk_ref, blk.at[a, pl.ds(0, orb)]),
                (inv_ref.at[q_at], blk.at[a, pl.ds(orb, q)]),
                (tiles_hbm, tiles_ref),
                (trial_hbm, trial_ref),
            )
        )
    ]
    for load in loads:
        load.start()
    wait_all = meet([w_peer(f) for f in range(1, nw)] + [c_peer(e) for e in range(1, nc)])
    loads[0].wait()
    loads[1].wait()
    wait_all()

    def has(s, side):
        return z - s >= 0 if side == 0 else z + s < nr

    def source(s, side):
        return z - s if side == 0 else z + s

    span = (orb + q) // PARTS

    def link(s, side, h):
        at = blk.at[source(s, side) * ng + x, pl.ds(h * span, span)]
        send, recv = (wu_s, wu_r) if side == 0 else (wd_s, wd_r)
        return lambda i: remote(
            at, at, send.at[i, h], recv.at[i, h], z_dev((z + 1) % nr if side == 0 else (z + nr - 1) % nr)
        )

    def pass_on(s, side, h):
        ahead = z + 1 < nr if side == 0 else z - 1 >= 0

        @pl.when(has(s, side) & ahead)
        def _():
            link(s, side, h)(s).start()

    def passed(s, side):
        ahead = z + 1 < nr if side == 0 else z - 1 >= 0

        @pl.when(has(s, side) & ahead)
        def _():
            for h in range(PARTS):
                link(s, side, h)(s).wait_send()

    def walk_x(zz, e, h):
        at = blk.at[zz * ng + x, pl.ds(h * span, span)]
        return remote(at, at, wx_s.at[e - 1, zz, h], wx_r.at[e - 1, zz, h], x_dev(e))

    def inverse_copy(s, f):
        return remote(
            blk.at[s, pl.ds(orb, q)],
            inv_all.at[s, q_at],
            iq_s.at[s, f - 1],
            iq_r.at[s, f - 1],
            c_peer(f),
        )

    def inverse(s):
        inv_all[s, q_at, :] = blk[s, pl.ds(orb, q), :]
        for f in range(1, nc):
            inverse_copy(s, f).start()

    def arrive(s, side, h):
        @pl.when(has(s, side))
        def _():
            link(s, side, h)(s - 1).wait_recv()

        if s < nr - 1:
            pass_on(s, side, h)

        @pl.when(has(s, side))
        def _():
            zz = source(s, side)
            for e in range(1, ng):
                walk_x(zz, e, h).start()
            if h == PARTS - 1:
                inverse(zz * ng + x)

    def tile_at(k, s):
        return tin.at[pl.ds(k * part, part), pl.ds(pl.multiple_of(s * slots, slots), slots), :]

    def cut_at(k, to):
        return cut.at[pl.ds(to * j_all + k * part, part)]

    tz = {}
    tx = {}

    def tile_z(k):
        for d in sorted(range(1, nr), key=lambda d: abs(d - nr / 2)):
            tz[k, d] = remote(
                cut_at(k, (z + d) % nr), tile_at(k, a), tz_s.at[k, d - 1], tz_r.at[k, d - 1], z_dev((z + d) % nr)
            )
            tz[k, d].start()

    def tile_x(k, d):
        at = tile_at(k, slab(d, 0))
        for e in range(1, ng):
            tx[k, d, e] = remote(
                cut_at(k, z) if d == 0 else at, at, tx_s.at[e - 1, k, d], tx_r.at[e - 1, k, d], x_dev(e)
            )
            tx[k, d, e].start()

    todo = list(range(chunks))

    def tile_event():
        if not todo or (todo[0], 1) not in tz:
            return
        k = todo.pop(0)
        for d in sorted(range(1, nr), key=lambda d: -abs(d - nr / 2)):
            tz[k, d].wait_recv()
            tile_x(k, d)

    for h in reversed(range(PARTS)):
        pass_on(0, 0, h)
        pass_on(0, 1, h)
        for e in range(1, ng):
            walk_x(z, e, h).start()
    inverse(a)
    loads[2].wait()

    def spread(i, carry):
        op32[pl.ds(i, tb, stride=slots), :] = tiles_ref[i].astype(f32)
        return carry

    def collect(p, carry):
        cut[p] = op32[pl.ds(pl.multiple_of(p * slots, slots), slots), :].astype(bf16)
        return carry

    lax.fori_loop(0, slots, spread, 0, unroll=2)
    lax.fori_loop(0, tb, collect, 0, unroll=4)
    for k in range(chunks * OWN_FIRST // 8):
        tile_x(k, 0)
    own_copy = pltpu.make_async_copy(
        cut.at[pl.ds(z * j_all, j_all)], tin.at[:, pl.ds(pl.multiple_of(a * slots, slots), slots), :], own_s
    )
    own_copy.start()
    loads[3].wait()

    def project(i, carry):
        out = lax.dot_general(
            tiles_ref[i], trial_ref[row_s[i]], (((0,), (0,)), ((), ())), preferred_element_type=f32
        )
        proj[i] = out.astype(bf16)
        return carry

    cuts = [slots * d // nr for d in range(nr + 1)]
    for s in range(1, nr):
        lax.fori_loop(cuts[s - 1], cuts[s], project, 0)
        for h in reversed(range(PARTS)):
            arrive(s, 0, h)
            arrive(s, 1, h)
        if s == min(2, nr - 1):
            for k in range(chunks * 2 // 8):
                tile_z(k)
    lax.fori_loop(cuts[nr - 1], cuts[nr], project, 0)
    for k in range(chunks * OWN_FIRST // 8, chunks):
        tile_x(k, 0)
    for k in range(chunks * 2 // 8, chunks * BEFORE // 8):
        tile_z(k)
    for _ in range(EVENTS[0]):
        tile_event()
    for e in range(1, ng):
        for zz in range(nr):
            if zz == nr // 2:
                for _ in range(EVENTS[1]):
                    tile_event()
            for h in range(PARTS):
                walk_x(zz, e, h).wait_recv()
            inverse(zz * ng + (x + ng - e) % ng)
    for _ in range(EVENTS[2]):
        tile_event()
    for s in range(nw):
        for f in range(1, nc):
            inverse_copy(s, f).wait_recv()

    def make_theta(j, carry):
        src = src_s[j]
        out = jnp.dot(blk[src, pl.ds(0, orb), :], inv_all[src], preferred_element_type=f32)
        theta[j] = out.astype(bf16).astype(f32).reshape(cols, tb, nel)
        return carry

    lax.fori_loop(0, walk_all, make_theta, 0)
    for _ in range(EVENTS[3]):
        tile_event()

    def score_tile(i, carry):
        tile = proj[i].astype(f32)
        column = col_s[i]

        def one(w, inner):
            value = (tile * theta[w, column]).reshape(tb // 8, 8, nel)
            value = jnp.sum(value, axis=0)
            lanes = value[:, :128]
            for n in range(128, nel, 128):
                lanes = lanes + value[:, n : n + 128]
            scores[w, pl.ds(i, 1), :] = jnp.sum(lanes, axis=0, keepdims=True)
            return inner

        lax.fori_loop(0, walk_all, one, 0, unroll=8)
        return carry

    lax.fori_loop(0, slots // 2, score_tile, 0)
    for _ in range(EVENTS[4]):
        tile_event()
    lax.fori_loop(slots // 2, slots, score_tile, 0)

    ones = jnp.ones((walk_all, 128), bf16)
    across = (((1,), (1,)), ((), ()))

    def dot2(value, other, flip):
        high = value.astype(bf16)
        low = (value - high.astype(f32)).astype(bf16)
        return sum(
            lax.dot_general(*((other, v) if flip else (v, other)), across, preferred_element_type=f32)
            for v in (high, low)
        )

    each = dot2(scores[...].reshape(walk_all * slots, 128), ones, True)
    lane = lax.broadcasted_iota(jnp.int32, each.shape, 1)
    keep = (lane // slots == lax.broadcasted_iota(jnp.int32, each.shape, 0)) & (
        lane % slots < count_s[0]
    )
    vec2 = jnp.concatenate([vec_ref[...]] * 2, axis=1)
    hot = (lax.broadcasted_iota(jnp.int32, (vec, 2 * slots), 0) == vec2).astype(f32).astype(bf16)
    hot = jnp.concatenate([hot] * (walk_all // 2), axis=1)
    bias_in[c] = dot2(jnp.where(keep, each, 0.0), hot, False)
    bias_copies = []
    for e in range(1, nc):
        at = bias_in.at[c]
        copy = remote(at, at, b_s.at[e - 1], b_r.at[e - 1], c_peer(e))
        copy.start()
        bias_copies.append(copy)
    for k in range(group):
        first = blk[src_s[k * ng + x], pl.ds(0, orb), :]
        term[0, k] = first.reshape(cols, nr, halves, ROWS, nel)
        for h in range(halves):
            total[k, h] = term[0, k, :, z, h].astype(f32).reshape(piece, nel)
    for _ in range(EVENTS[5]):
        tile_event()
    for copy in bias_copies:
        copy.wait_recv()
    force = bias_in[0]
    for e in range(1, nc):
        force = force + bias_in[e]
    force_ref[...] = force
    field = (noise_ref[...] - SQRT_TAU * force).astype(bf16)
    lane2 = lax.broadcasted_iota(jnp.int32, (vec, 2 * slots), 1)
    mine = lane2 // slots == a % 2
    fits = (lane2 % slots < count_s[0]) & mine
    hot2 = jnp.where(
        fits & (lax.broadcasted_iota(jnp.int32, (vec, 2 * slots), 0) == vec2), 1.0, 0.0
    ).astype(bf16)
    tile_rows = row_ref[...]
    block = tile_rows // cols
    spot = ((block % 2) * ny + block // 2) * cols + tile_rows % cols
    place2 = jnp.concatenate([col_ref[...] * rblocks + spot] * 2, axis=1)
    spots = jnp.where(mine[:8], place2.astype(f32), 0.0)
    for g in range(ng):
        pick = lax.broadcasted_iota(jnp.int32, (pad, walk_all), 1) == (
            lax.broadcasted_iota(jnp.int32, (pad, walk_all), 0) * ng + g
        )
        fields = jnp.dot(pick.astype(f32).astype(bf16), field, preferred_element_type=f32)
        coeff = jnp.dot(fields.astype(bf16), hot2, preferred_element_type=f32)
        sent[g] = jnp.concatenate([coeff, spots], axis=0).astype(bf16)
    sent_copies = []
    for f in range(1, nw):
        copy = remote(
            sent.at[((a + f) % nw) % ng], got.at[a], g_s.at[f - 1], g_r.at[f - 1], w_peer(f)
        )
        copy.start()
        sent_copies.append(copy)
    got[a] = sent[x]
    for k in range(chunks * BEFORE // 8, chunks):
        tile_z(k)
    for _ in range(EVENTS[6]):
        tile_event()
    for copy in sent_copies:
        copy.wait_recv()

    def lanes(at):
        return jnp.concatenate(
            [got[2 * p].astype(f32)[at : at + 1] + got[2 * p + 1].astype(f32)[at : at + 1] for p in range(nw // 2)],
            axis=1,
        )

    hit = lax.broadcasted_iota(jnp.int32, (places, depth), 0) == lanes(pad).astype(jnp.int32)
    for w in range(group):
        wts[pl.ds(w * places, places), :] = jnp.where(hit, lanes(w), 0.0).astype(bf16)

    def op_at(h, w, col):
        return ((h * group + w) * cols + col) * rows

    def build(h):
        def one(j, carry):
            out = jnp.dot(wts[...], tin[j], preferred_element_type=f32)
            for w in range(group):
                for col in range(cols):
                    top = w * places + col * rblocks
                    at = op_at(h, w, col) + j - h * ROWS
                    op32[pl.ds(at, rblocks, stride=ROWS), :] = out[top : top + rblocks]
            return carry

        return one

    def build_chunk(k):
        for d in range(nr):
            for e in range(1, ng):
                tx[k, d, e].wait_recv()
        lax.fori_loop(k * part, (k + 1) * part, build(k * part // ROWS), 0)

    def narrow(h):
        for w in range(group):
            for col in range(cols):
                op[h, w, :, pl.ds(col * tb, tb)] = op32[pl.ds(op_at(h, w, col), rows), :].astype(bf16)

    items = [(0, w, h) for h in range(halves) for w in range(group)]
    items += [(k, w, h) for k in range(1, TAYLOR) for w in range(group) for h in range(halves)]
    spots_of = {item: t for t, item in enumerate(items)}
    waited = set()
    core_copy = {}
    y_copy = {}
    z_copy = {}

    def multiply(t):
        k, w, h = items[t]
        if k and (w, k) not in waited:
            waited.add((w, k))
            for g in range(halves):
                for d in range(1, nr):
                    z_wait(spots_of[k - 1, w, g], d)
        right = term[k, w].reshape(orb, nel)
        there = pl.ds(pl.multiple_of((1 - core) * half, half), half)
        here = pl.ds(pl.multiple_of(core * half, half), half)
        c_send[t] = jnp.dot(op[h, w, there, :], right, preferred_element_type=f32).astype(bf16)
        core_copy[t] = remote(
            c_send.at[t], c_recv.at[t], cs.at[t], cr.at[t], c_dev(y * 2 + 1 - core)
        )
        core_copy[t].start()
        own[t % 4] = jnp.dot(op[h, w, here, :], right, preferred_element_type=f32)

    def add_core(t):
        core_copy[t].wait_recv()
        for e in range(1, ny):
            to = (y + e) % ny
            at = pl.ds(pl.multiple_of(to * piece, piece), piece)
            y_send[t, e - 1] = (own[t % 4, at, :] + c_recv[t, at, :].astype(f32)).astype(bf16)
            y_copy[t, e] = remote(
                y_send.at[t, e - 1], y_recv.at[t, e - 1], ys.at[t, e - 1], yr.at[t, e - 1], c_dev(to * 2 + core)
            )
            y_copy[t, e].start()

    def relay(t):
        k, w, h = items[t]
        if k == TAYLOR - 1 or nr < 3:
            return
        for at_z, from_z, d in ((nr - 2, 0, nr - 2), (1, nr - 1, 2)):

            @pl.when(z == at_z)
            def _():
                z_send(t, d, from_z).wait_recv()
                relay_copy(t, from_z).start()

            later(z == at_z, lambda from_z=from_z: relay_copy(t, from_z).wait_send())

    def relay_copy(t, from_z):
        k, w, h = items[t]
        at = term.at[k + 1, w, :, from_z, h]
        d = nr - 1 if from_z == 0 else 1
        return remote(at, at, zs.at[k, w, h, nr - 1], zr.at[k, w, h, d - 1], z_dev(nr - 1 - from_z))

    def z_send(t, d, from_z):
        k, w, h = items[t]
        at = term.at[k + 1, w, :, from_z, h]
        return remote(at, at, zs.at[k, w, h, d - 1], zr.at[k, w, h, d - 1], z_dev((from_z + d) % nr))

    def far(d, sender):
        if nr < 3:
            return False
        if d == nr - 1:
            return sender == 0
        if d == 1:
            return sender == nr - 1
        return False

    def z_wait(t, d):
        here = (z + nr - d) % nr
        taken = False
        if nr >= 3:
            if d == nr - 2:
                taken = z == nr - 2
            if d == 2:
                taken = (z == 1) if taken is False else taken | (z == 1)
        if taken is False:
            z_send(t, d, here).wait_recv()
        else:

            @pl.when(jnp.logical_not(taken))
            def _():
                z_send(t, d, here).wait_recv()

    def finish(t):
        k, w, h = items[t]
        at = pl.ds(pl.multiple_of(y * piece, piece), piece)
        value = own[t % 4, at, :] + c_recv[t, at, :].astype(f32)
        for e in range(1, ny):
            y_copy[t, e].wait_recv()
            value = value + y_recv[t, e - 1].astype(f32)
        new = (SQRT_TAU / (k + 1) * value).astype(bf16)
        added = total[w, h] + new.astype(f32)
        if k < TAYLOR - 1:
            total[w, h] = added
            term[k + 1, w, :, z, h] = new.reshape(cols, ROWS, nel)
            for d in sorted(range(1, nr), key=lambda d: abs(d - nr / 2)):
                skip = far(d, z)
                if skip is False:
                    z_send(t, d, z).start()
                    later(None, lambda d=d: z_send(t, d, z).wait_send())
                else:

                    @pl.when(jnp.logical_not(skip))
                    def _():
                        z_send(t, d, z).start()

                    later(jnp.logical_not(skip), lambda d=d: z_send(t, d, z).wait_send())
            return
        fin[w, h] = added.astype(bf16).reshape(cols, ROWS, nel)

        @pl.when(z == w)
        def _():
            out_ref[:, z, h] = fin[w, h]

        @pl.when(z != w)
        def _():
            remote(fin.at[w, h], out_ref.at[:, z, h], fs.at[w, h], fr.at[z, h], z_dev(w)).start()

    def run(first, last, tail):
        for t in range(first, last + LAG_RELAY):
            if first <= t - LAG_RELAY:
                relay(t - LAG_RELAY)
            if t < last:
                multiply(t)
            if first <= t - LAG_CORE < last:
                add_core(t - LAG_CORE)
            if first <= t - LAG_Y < last:
                finish(t - LAG_Y)
        return []

    tile_event()
    own_copy.wait()
    per = ROWS // part
    behind = []
    for h in range(halves):
        for k in range(h * per, (h + 1) * per):
            while todo and k >= todo[0]:
                tile_event()
            build_chunk(k)
            tile_event()
            if behind:
                relay(behind.pop(0))
        narrow(h)
        for t in behind:
            relay(t)
        behind = []
        if h < halves - 1:
            behind = run(h * group, (h + 1) * group, False)
    run((halves - 1) * group, len(items), True)
    for w in range(group):

        @pl.when(z != w)
        def _():
            for h in range(halves):
                copy = remote(fin.at[w, h], out_ref.at[:, w, h], fs.at[w, h], fr.at[w, h], z_dev(w))
                copy.wait_send()
                copy.wait_recv()

    for s in range(nr - 1):
        passed(s, 0)
        passed(s, 1)
    for zz in range(nr):
        for e in range(1, ng):
            for h in range(PARTS):
                walk_x(zz, e, h).wait_send()
    for s in range(nw):
        for f in range(1, nc):
            inverse_copy(s, f).wait_send()
    for copy in list(tz.values()) + list(tx.values()) + bias_copies + sent_copies:
        copy.wait_send()
    for copy in list(core_copy.values()) + list(y_copy.values()):
        copy.wait_send()
    for condition, action in ends:
        if condition is None:
            action()
        else:
            pl.when(condition)(action)


def step(row, col, vector, count, sources, walkers, inv, trial, tiles, noise, nr, ng, nc):
    f32 = jnp.float32
    bf16 = jnp.bfloat16
    nw = nr * ng
    orb, nel = walkers.shape
    slots, tb, _ = tiles.shape
    walk_all, vec = noise.shape
    group = walk_all // ng
    cols = orb // tb
    q = nel // nc
    pad = (group + 7) // 8 * 8
    j = tb // nr
    chunks = j // CHUNK
    rblocks = trial.shape[0]
    halves = j // ROWS
    rows = rblocks * ROWS
    piece = rows // nc
    more = max(nc // 2 - 1, 1)
    items = TAYLOR * group * halves
    dma = pltpu.SemaphoreType.DMA
    vmem = pl.BlockSpec(memory_space=pltpu.VMEM)
    smem = pl.BlockSpec(memory_space=pltpu.SMEM)
    hbm = pl.BlockSpec(memory_space=pl.ANY)

    def both(*shape):
        return [dma(shape), dma(shape)]

    return pl.pallas_call(
        functools.partial(step_kernel, nr, ng, nc),
        out_shape=(
            jax.ShapeDtypeStruct((walk_all, vec), f32),
            jax.ShapeDtypeStruct((cols, nr, halves, ROWS, nel), bf16),
        ),
        in_specs=[smem] * 4 + [hbm] * 4 + [vmem] * 4,
        out_specs=(vmem, vmem),
        scratch_shapes=[
            pltpu.VMEM((nw, orb + q, nel), bf16),
            pltpu.VMEM((nw, nel, nel), bf16),
            pltpu.VMEM((slots, tb, nel), bf16),
            pltpu.VMEM((walk_all, cols, tb, nel), f32),
            pltpu.VMEM((walk_all, slots, 128), f32),
            pltpu.VMEM((nc, walk_all, vec), f32),
            pltpu.VMEM((ng, pad + 8, 2 * slots), bf16),
            pltpu.VMEM((nw, pad + 8, 2 * slots), bf16),
            pltpu.VMEM((j, nw * slots, tb), bf16),
            pltpu.VMEM((group * cols * rblocks, nw * slots), bf16),
            pltpu.VMEM((max(halves * group * cols * rows, slots * tb) + max(ROWS, slots), tb), f32),
            pltpu.VMEM((halves, group, rows, orb), bf16),
            pltpu.VMEM((TAYLOR, group, cols, nr, halves, ROWS, nel), bf16),
            pltpu.VMEM((group, halves, piece, nel), f32),
            pltpu.VMEM((4, rows // 2, nel), f32),
            pltpu.VMEM((items, rows // 2, nel), bf16),
            pltpu.VMEM((items, rows // 2, nel), bf16),
            pltpu.VMEM((items, more, piece, nel), bf16),
            pltpu.VMEM((items, more, piece, nel), bf16),
            pltpu.VMEM((group, halves, cols, ROWS, nel), bf16),
            pltpu.VMEM(trial.shape, bf16),
            pltpu.VMEM(tiles.shape, bf16),
            pltpu.VMEM((tb, slots, tb), bf16),
            dma((4,)),
        ]
        + both(nr - 1, PARTS)
        + both(nr - 1, PARTS)
        + both(ng - 1, nr, PARTS)
        + both(nw, nc - 1)
        + both(chunks, nr - 1)
        + both(ng - 1, chunks, nr)
        + [dma]
        + both(nc - 1)
        + both(nw - 1)
        + both(items)
        + both(items, more)
        + both(TAYLOR - 1, group, halves, nr)
        + both(group, halves),
        compiler_params=pltpu.CompilerParams(
            collective_id=0, has_side_effects=True, vmem_limit_bytes=VMEM_LIMIT
        ),
    )(
        row,
        col,
        count,
        sources,
        walkers,
        inv,
        trial,
        tiles,
        noise,
        vector.reshape(1, slots),
        row.reshape(1, slots),
        col.reshape(1, slots),
    )


def settle_kernel(force_in, out_in, force_out, out_out):
    force_out[...] = force_in[...]
    out_out[...] = out_in[...]


def settle(force, out):
    vmem = pl.BlockSpec(memory_space=pltpu.VMEM)
    return pl.pallas_call(
        settle_kernel,
        out_shape=tuple(jax.ShapeDtypeStruct(v.shape, v.dtype) for v in (force, out)),
        in_specs=[vmem] * 2,
        out_specs=(vmem,) * 2,
    )(force, out)


def body(
    walkers,
    intersection_inv,
    trial_state,
    chol_tiles,
    tile_vector,
    tile_row,
    tile_col,
    tile_count,
    sources,
    aux_noise,
):
    _, orb, nel = walkers.shape
    tb = chol_tiles.shape[1]
    rblocks = trial_state.shape[0] // tb
    wide = lax.axis_size("wide")
    nc = lax.axis_size("chol")
    nr, ng = split_wide(wide, tb)
    force, out = step(
        tile_row,
        tile_col,
        tile_vector,
        tile_count,
        sources,
        walkers[0],
        intersection_inv[0],
        trial_state.reshape(rblocks, tb, nel),
        chol_tiles,
        aux_noise,
        nr,
        ng,
        nc,
    )
    return settle(force, out.reshape(1, orb, nel))


def solution(mesh):
    return jax.shard_map(
        body,
        mesh=mesh,
        in_specs=(
            P("wide", "chol", None),
            P("wide", None, None),
            P(),
            P(("wide", "chol"), None, None),
            P(("wide", "chol")),
            P(("wide", "chol")),
            P(("wide", "chol")),
            P(("wide", "chol")),
            P(),
            P(None, "wide"),
        ),
        out_specs=(P(None, "wide"), P("wide", "chol", None)),
        check_vma=False,
    )
```
